512 devices in a mesh: src: 64 (over z, x), tm: 8 (over y, core).
Axes of the slice: x: 4, y: 4, z: 16, core: 2. Of those that a mesh axis runs over, the one named last changes fastest.
Arguments:
- left_vector: float32 [8, 131072], P(None, ('src', 'tm')), may hold values from -12 to 12
- source_coeffs: float32 [5, 8, 131072], P(None, None, ('src', 'tm')), may hold values from -1.5 to 1.5
- knot_coeffs: float32 [12, 8, 131072], P(None, None, ('src', 'tm')), may hold values from -1.5 to 1.5
- source_index: int32 [8, 131072], P(None, ('src', 'tm')), may hold values from 0 to 1023
- band_start: int32 [8, 131072], P(None, ('src', 'tm')), may hold values from 0 to 4095, as said below
- bucket_fill: int32 [8, 512], P(None, ('src', 'tm')), may hold values from 51 to 256, as said below
- source_vector: float32 [5, 524288], P(None, ('src', 'tm')), may hold values from -6 to 6
- knot_vector: float32 [3, 8, 16384], P(None, 'tm', 'src'), may hold values from -6 to 6
- source_search: float32 [5, 524288], P(None, ('src', 'tm')), may hold values from -6 to 6
- knot_search: float32 [3, 8, 16384], P(None, 'tm', 'src'), may hold values from -6 to 6
- source_solution: float32 [5, 524288], P(None, ('src', 'tm')), may hold values from -6 to 6
- knot_solution: float32 [3, 8, 16384], P(None, 'tm', 'src'), may hold values from -6 to 6
- recurrence: float32 [3], replicated, may hold values from 0.5 to 1.5
Outputs:
- left_next: float32 [8, 131072], P(None, ('src', 'tm'))
- source_next: float32 [5, 524288], P(None, ('src', 'tm'))
- knot_next: float32 [3, 8, 16384], P(None, 'tm', 'src')
- search_source: float32 [5, 524288], P(None, ('src', 'tm'))
- search_knot: float32 [3, 8, 16384], P(None, 'tm', 'src')
- solution_source: float32 [5, 524288], P(None, ('src', 'tm'))
- solution_knot: float32 [3, 8, 16384], P(None, 'tm', 'src')
- recurrence_next: float32 [4], replicated
The draws below stay inside these ranges and needn't reach their ends.
Inputs may be any that keep to these rules, and one draw needn't show every extreme that they name: `bucket_fill`: in every draw one bucket of some group block holds exactly 256 observations. Call band_start // 64 the knot owner of a slot. Among the 8 x 256 slots of one column block of 256, each knot owner is named at most 64 times, and in every block some owner exactly 64 times.
All inputs are finite; a program needn't handle non-finite values.
Results may differ from the reference program's by a relative error of at most 0.00002.
Values sent between devices are 32-bit elements; how exact they have to be, the bound alone decides.
A program may use at most 64 MiB of HBM per device.

```python
import jax
import jax.numpy as jnp
from jax import lax

SRC_DEV = 1024
CAP = 256
KNOT_DEV = 256
KB = 4
SOURCES = 524288
NOBS_COL = 131072
KNOTS_SLAB = 16384
N_SRC = 64
N_TM = 8


def draw_left_vector(key, part):
    blocks = NOBS_COL // CAP
    rank = (jnp.arange(NOBS_COL) // CAP).astype(jnp.float32) / max(blocks - 1, 1)
    base = jax.random.normal(key, (N_TM, NOBS_COL), jnp.float32)
    scale = 1.0 + 2.0 * rank
    values = base * scale[None, :]
    return jnp.clip(values, -12.0, 12.0)


def draw_bucket_fill(key, part):
    blocks = NOBS_COL // CAP
    fill = jax.random.randint(key, (N_TM * blocks,), CAP // 5, CAP + 1)
    chosen = jax.random.randint(jax.random.fold_in(key, 7), (), 0, N_TM * blocks)
    fill = jnp.where(jnp.arange(N_TM * blocks) == chosen, CAP, fill)
    return fill.reshape(N_TM, blocks).astype(jnp.int32)


def band_block(block_key):
    local_slots = N_TM * CAP
    half_most = local_slots // N_SRC
    bands_owner = KNOT_DEV // KB
    key_slots, key_owner, key_coin, key_band = jax.random.split(block_key, 4)
    bucket = jax.random.permutation(key_slots, local_slots) // half_most
    owners = jax.random.permutation(key_owner, N_SRC)
    coins = jax.random.randint(key_coin, (N_SRC,), 0, 2)
    coins = coins.at[0].set(1).at[1].set(0)
    target = jnp.where(coins[bucket] == 1, owners[(bucket + 1) % N_SRC], owners[bucket])
    local_band = jax.random.randint(key_band, (local_slots,), 0, bands_owner)
    return (target * bands_owner + local_band).astype(jnp.int32).reshape(N_TM, CAP)


def draw_band_start(key, part):
    blocks = NOBS_COL // CAP
    block_keys = jax.random.split(jax.random.fold_in(key, 11), blocks)
    drawn = jax.vmap(band_block)(block_keys)
    return jnp.transpose(drawn, (1, 0, 2)).reshape(N_TM, NOBS_COL).astype(jnp.int32)


def place_ends(values, own_key, smallest, high):
    spot = [jax.random.randint(jax.random.fold_in(own_key, axis), (), 0, length) for axis, length in enumerate(values.shape)]
    longest = values.shape.index(max(values.shape))
    next_to = spot[:longest] + [(spot[longest] + 1) % values.shape[longest]] + spot[longest + 1:]
    return values.at[tuple(spot)].set(smallest).at[tuple(next_to)].set(high)


def level_of(own_key, extent, pieces, least, high):
    factor_of = 1.0
    for position, blocks in pieces:
        draws = jax.random.uniform(jax.random.fold_in(jax.random.fold_in(own_key, 6), position), (blocks,), jnp.float32, least / len(pieces), high / len(pieces))
        factor_of = factor_of * jnp.repeat(jnp.exp(draws), extent[position] // blocks).reshape((-1,) + (1,) * (len(extent) - 1 - position))
    return factor_of


def gaussian(rng, shape, deviation, reach, shards=(), held_as=jnp.bfloat16):
    values = deviation * jax.random.normal(rng, shape, jnp.float32)
    if shards:
        values = values * level_of(rng, shape, shards, -0.22, 0.18)
    return jnp.clip(values, -reach, reach).astype(held_as)


def setup_inputs(seed: int = 0) -> dict:
    streams_of = jax.random.split(jax.random.key(seed), 14)
    return {
        "left_vector": draw_left_vector(jax.random.fold_in(streams_of[13], 71), 0),
        "source_coeffs": gaussian(streams_of[1], (5, N_TM, NOBS_COL), 0.25, 1.5, ((2, 512),), jnp.float32),
        "knot_coeffs": gaussian(streams_of[2], (3 * KB, N_TM, NOBS_COL), 0.25, 1.5, ((2, 512),), jnp.float32),
        "source_index": place_ends(jax.random.randint(streams_of[3], (N_TM, NOBS_COL), 0, SRC_DEV), jax.random.fold_in(streams_of[3], 1), 0, SRC_DEV - 1).astype(jnp.int32),
        "band_start": draw_band_start(jax.random.fold_in(streams_of[13], 71), 0),
        "bucket_fill": draw_bucket_fill(jax.random.fold_in(streams_of[13], 71), 0),
        "source_vector": gaussian(streams_of[6], (5, SOURCES), 1.0, 6.0, ((1, 512),), jnp.float32),
        "knot_vector": gaussian(streams_of[7], (3, N_TM, KNOTS_SLAB), 1.0, 6.0, ((1, 8), (2, 64)), jnp.float32),
        "source_search": gaussian(streams_of[8], (5, SOURCES), 1.0, 6.0, ((1, 512),), jnp.float32),
        "knot_search": gaussian(streams_of[9], (3, N_TM, KNOTS_SLAB), 1.0, 6.0, ((1, 8), (2, 64)), jnp.float32),
        "source_solution": gaussian(streams_of[10], (5, SOURCES), 1.0, 6.0, ((1, 512),), jnp.float32),
        "knot_solution": gaussian(streams_of[11], (3, N_TM, KNOTS_SLAB), 1.0, 6.0, ((1, 8), (2, 64)), jnp.float32),
        "recurrence": jnp.clip(jax.random.uniform(streams_of[12], (3,), jnp.float32, 0.5, 1.5), 0.5, 1.5),
    }


EPSILON = 1e-06

def regroup(values):
    shaped = values.reshape(N_TM, N_SRC, N_TM, CAP)
    return jnp.transpose(shaped, (2, 1, 0, 3)).reshape(N_TM, NOBS_COL)

def reference(left_vector, source_coeffs, knot_coeffs, source_index, band_start, bucket_fill, source_vector, knot_vector, source_search, knot_search, source_solution, knot_solution, recurrence):
    total_obs = N_TM * NOBS_COL
    unknowns = 5 * SOURCES + 3 * N_TM * KNOTS_SLAB
    ratio = unknowns / total_obs
    alpha = recurrence[0]
    pivot = recurrence[1]
    remainder = recurrence[2]
    column = lax.broadcasted_iota(jnp.int32, (N_TM, NOBS_COL), 1)
    block = column // CAP
    valid = (column % CAP < jnp.repeat(bucket_fill, CAP, axis=1)).astype(jnp.float32)
    source_of = (block * SRC_DEV + source_index).astype(jnp.int32)
    slab_of = (block % N_TM).astype(jnp.int32)
    first_knot = (band_start * KB).astype(jnp.int32)
    image = jnp.zeros((N_TM, NOBS_COL), jnp.float32)
    for k in range(5):
        image = image + source_coeffs[k] * source_vector[k][source_of]
    knot_image = jnp.zeros((N_TM, NOBS_COL), jnp.float32)
    for row in range(3 * KB):
        axis_id = row // KB
        offset = row % KB
        knot_image = knot_image + knot_coeffs[row] * knot_vector[axis_id][slab_of, (first_knot + offset).astype(jnp.int32)]
    raw = valid * (image + regroup(knot_image) - alpha * left_vector)
    beta = jnp.sqrt(jnp.sum(raw * raw) / total_obs + EPSILON)
    left_next = raw / beta
    left_slab = regroup(left_next)
    gradient_source = jnp.zeros((5, SOURCES), jnp.float32).at[:, source_of.reshape(-1)].add((source_coeffs * left_next[None]).reshape(5, -1))
    gradient_knot = jnp.zeros((3, N_TM, KNOTS_SLAB), jnp.float32)
    for row in range(3 * KB):
        axis_id = row // KB
        offset = row % KB
        gradient_knot = gradient_knot.at[axis_id, slab_of, (first_knot + offset).astype(jnp.int32)].add(knot_coeffs[row] * left_slab)
    source_raw = ratio * gradient_source - beta * source_vector
    knot_raw = ratio * gradient_knot - beta * knot_vector
    alpha_next = jnp.sqrt((jnp.sum(source_raw * source_raw) + jnp.sum(knot_raw * knot_raw)) / unknowns + EPSILON)
    source_next = source_raw / alpha_next
    knot_next = knot_raw / alpha_next
    radius = jnp.sqrt(pivot * pivot + beta * beta)
    cosine = pivot / radius
    sine = beta / radius
    coupling = sine * alpha_next
    step_gain = cosine * remainder
    solution_source = source_solution + step_gain / radius * source_search
    solution_knot = knot_solution + step_gain / radius * knot_search
    search_source = source_next - coupling / radius * source_search
    search_knot = knot_next - coupling / radius * knot_search
    recurrence_next = jnp.stack([alpha_next, beta, -cosine * alpha_next, sine * remainder])
    return (left_next, source_next, knot_next, search_source, search_knot, solution_source, solution_knot, recurrence_next)
```

```python
import functools

import jax
import jax.numpy as jnp
from jax import lax
from jax.experimental import pallas as pl
from jax.experimental.pallas import tpu as pltpu
from jax.sharding import PartitionSpec as P

KB = 4
EPSILON = 1e-06
F32 = jnp.float32
BF16 = jnp.bfloat16
NT = (((1,), (1,)), ((), ()))
NN = (((1,), (0,)), ((), ()))


def split3(x):
    hi = x.astype(BF16)
    rest = x - hi.astype(F32)
    mid = rest.astype(BF16)
    low = (rest - mid.astype(F32)).astype(BF16)
    return hi, mid, low


def split3_f32(x):
    return [part.astype(F32) for part in split3(x)]


def iterate(
    n_src,
    n_tm,
    total_obs,
    unknowns,
    left_ref,
    sc_ref,
    kc_ref,
    si_ref,
    bs_ref,
    fill_ref,
    sv_ref,
    kv_ref,
    rec_ref,
    raw_out,
    sraw_out,
    kraw_out,
    scal_out,
    ag,
    pbuf,
    prcv,
    rbuf,
    rrcv,
    rs_send,
    rs_recv,
    ar1a,
    ar1b,
    ar2a,
    ar2b,
    ohs,
    ohk,
    acc,
    tsend,
    ssem,
    agr,
    prr,
    rrr,
    rsr,
    ar1ar,
    ar1br,
    ar2ar,
    ar2br,
    agss,
    prs,
    rrs,
    rss,
    ar1as,
    ar1bs,
    ar2as,
    ar2bs,
):
    s = lax.axis_index("src")
    m = lax.axis_index("tm")
    ratio = unknowns / total_obs
    cap = left_ref.shape[1]

    def each(n, f):
        lax.fori_loop(1, n, lambda d, c: (f(d), c)[1], 0)

    def src_copy(d, src, dst, send, recv):
        o = lax.rem(s + d, n_src)
        return pltpu.make_async_remote_copy(
            src_ref=src(o),
            dst_ref=dst,
            send_sem=send.at[d],
            recv_sem=recv.at[s],
            device_id={"src": o},
            device_id_type=pl.DeviceIdType.MESH,
        )

    def src_arrival(d, dst, send, recv):
        o = lax.rem(s + d, n_src)
        return pltpu.make_async_remote_copy(
            src_ref=dst(o),
            dst_ref=dst(o),
            send_sem=send.at[d],
            recv_sem=recv.at[o],
            device_id={"src": o},
            device_id_type=pl.DeviceIdType.MESH,
        )

    def tm_copy(d, src, dst, send, recv):
        o = lax.rem(m + d, n_tm)
        return pltpu.make_async_remote_copy(
            src_ref=src(o),
            dst_ref=dst,
            send_sem=send.at[d],
            recv_sem=recv.at[m],
            device_id={"tm": o},
            device_id_type=pl.DeviceIdType.MESH,
        )

    def tm_arrival(d, dst, send, recv):
        o = lax.rem(m + d, n_tm)
        return pltpu.make_async_remote_copy(
            src_ref=dst(o),
            dst_ref=dst(o),
            send_sem=send.at[d],
            recv_sem=recv.at[o],
            device_id={"tm": o},
            device_id_type=pl.DeviceIdType.MESH,
        )

    barrier = pltpu.get_barrier_semaphore()

    def greet_src(d):
        pl.semaphore_signal(
            barrier, inc=1, device_id={"src": lax.rem(s + d, n_src)}, device_id_type=pl.DeviceIdType.MESH
        )

    def greet_tm(d):
        pl.semaphore_signal(
            barrier, inc=1, device_id={"tm": lax.rem(m + d, n_tm)}, device_id_type=pl.DeviceIdType.MESH
        )

    each(n_src, greet_src)
    each(n_tm, greet_tm)

    for a in range(3):
        for sub in range(2):
            ag[s, a * 2 + sub : a * 2 + sub + 1, :] = kv_ref[a, :, sub * 128 : (sub + 1) * 128]

    alpha = rec_ref[0]
    pad3 = jnp.zeros((3, 128), F32)
    table = jnp.concatenate(
        [jnp.concatenate([sv_ref[:, l * 128 : (l + 1) * 128], pad3], axis=0) for l in range(8)], axis=0
    )
    stable = jnp.concatenate(split3(table), axis=1)
    rows128 = lax.broadcasted_iota(jnp.int32, (128, cap), 0)
    lane = lax.broadcasted_iota(jnp.int32, (1, cap), 1)

    for t in range(n_tm):
        idx = si_ref[t : t + 1, :]
        hi = jnp.bitwise_and(idx, 127)
        lo = jnp.right_shift(idx, 7)
        oh = jnp.where(rows128 == hi, 1.0, 0.0).astype(BF16)
        ohs[t] = oh
        found = lax.dot_general(
            stable, jnp.concatenate([oh, oh, oh], axis=0), NN, preferred_element_type=F32
        )
        picked = jnp.zeros((8, cap), F32)
        for l in range(8):
            picked = picked + jnp.where(lo == l, found[l * 8 : (l + 1) * 8], 0.0)
        coef = sc_ref[:, t, :]
        image = jnp.sum(coef * picked[0:5], axis=0, keepdims=True)
        pbuf[t, 0:1, :] = image - alpha * left_ref[t : t + 1, :]
        pbuf[t, 1:2, :] = jnp.where(lane < fill_ref[t : t + 1, :], 1.0, 0.0)

    pl.semaphore_wait(barrier, n_src + n_tm - 2)

    each(n_src, lambda d: src_copy(d, lambda o: ag.at[s, pl.ds(0, 6)], ag.at[s, pl.ds(0, 6)], agss, agr).start())
    each(n_tm, lambda d: tm_copy(d, lambda o: pbuf.at[o], prcv.at[m], prs, prr).start())
    prcv[m] = pbuf[m]

    for i in range(n_tm):
        band = bs_ref[i : i + 1, :]
        hi = jnp.bitwise_and(jnp.right_shift(band, 5), 1) * 64 + jnp.right_shift(band, 6)
        ohk[i] = jnp.where(rows128 == hi, 1.0, 0.0).astype(BF16)

    each(n_tm, lambda d: tm_arrival(d, lambda o: prcv.at[o], prs, prr).wait_recv())
    each(n_src, lambda d: src_arrival(d, lambda o: ag.at[o, pl.ds(0, 6)], agss, agr).wait_recv())

    parts = []
    for a in range(3):
        whole = jnp.concatenate([ag[:, a * 2 + sub, :] for sub in range(2)], axis=0)
        parts.append(jnp.concatenate(split3(jnp.transpose(whole)), axis=1))
    ktable = jnp.concatenate(parts, axis=0)

    band_rows = jnp.right_shift(rows128, 2)
    total = jnp.zeros((1, cap), F32)
    acc[...] = jnp.zeros_like(acc)
    for i in range(n_tm):
        oh = ohk[i]
        found = lax.dot_general(
            ktable, jnp.concatenate([oh, oh, oh], axis=0), NN, preferred_element_type=F32
        )
        lo = jnp.bitwise_and(bs_ref[i : i + 1, :], 31)
        hit = band_rows == lo
        coefs = []
        mixed = None
        for a in range(3):
            four = kc_ref[a * 4 : a * 4 + 4, i, :]
            eight = jnp.concatenate([four, four], axis=0)
            coefs.append(eight)
            term = found[a * 128 : (a + 1) * 128].reshape(16, 8, cap) * eight[None]
            mixed = term if mixed is None else mixed + term
        image = jnp.sum(jnp.where(hit, mixed.reshape(128, cap), 0.0), axis=0, keepdims=True)
        raw = prcv[i, 1:2, :] * (prcv[i, 0:1, :] + image)
        rbuf[i] = raw
        total = total + raw * raw
        hit_b = jnp.where(hit, 1.0, 0.0).astype(BF16)
        spread = [[], [], []]
        for a in range(3):
            for q, part in enumerate(split3_f32(coefs[a] * raw)):
                two = jnp.concatenate([part, part], axis=0).astype(BF16)
                spread[q].append(hit_b * jnp.concatenate([two] * 8, axis=0))
        terms = jnp.concatenate([jnp.concatenate(rows, axis=0) for rows in spread], axis=1)
        acc[...] += lax.dot_general(
            terms, jnp.concatenate([oh, oh, oh], axis=1), NT, preferred_element_type=F32
        )

    ar1a[s] = jnp.broadcast_to(jnp.sum(total, axis=1, keepdims=True), (1, 128))
    for a in range(3):
        turned = jnp.transpose(acc[a * 128 : (a + 1) * 128, :])
        for sub in range(2):
            rs_send[:, a * 2 + sub, :] = turned[sub * 64 : (sub + 1) * 64]

    each(n_tm, lambda d: tm_copy(d, lambda o: rbuf.at[o], rrcv.at[m], rrs, rrr).start())
    rrcv[m] = rbuf[m]
    each(n_src, lambda d: src_copy(d, lambda o: ar1a.at[s], ar1a.at[s], ar1as, ar1ar).start())
    each(n_src, lambda d: src_copy(d, lambda o: rs_send.at[o, pl.ds(0, 6)], rs_recv.at[s, pl.ds(0, 6)], rss, rsr).start())
    rs_recv[s] = rs_send[s]

    each(n_tm, lambda d: tm_arrival(d, lambda o: rrcv.at[o], rrs, rrr).wait_recv())
    grad = jnp.zeros((64, 128), F32)
    for t in range(n_tm):
        raw = rrcv[t]
        raw_out[t : t + 1, :] = raw
        lo = jnp.right_shift(si_ref[t : t + 1, :], 7)
        coef = jnp.concatenate([sc_ref[:, t, :], jnp.zeros((3, cap), F32)], axis=0)
        spread = []
        for part in split3_f32(coef * raw):
            spread.append(
                jnp.concatenate([jnp.where(lo == l, part, 0.0) for l in range(8)], axis=0).astype(BF16)
            )
        oh = ohs[t]
        grad = grad + lax.dot_general(
            jnp.concatenate(spread, axis=1),
            jnp.concatenate([oh, oh, oh], axis=1),
            NT,
            preferred_element_type=F32,
        )

    each(n_src, lambda d: src_arrival(d, lambda o: ar1a.at[o], ar1as, ar1ar).wait_recv())
    ar1b[m] = jnp.sum(ar1a[...], axis=0)
    each(n_tm, lambda d: tm_copy(d, lambda o: ar1b.at[m], ar1b.at[m], ar1bs, ar1br).start())
    each(n_tm, lambda d: tm_arrival(d, lambda o: ar1b.at[o], ar1bs, ar1br).wait_recv())
    beta = jnp.sqrt(jnp.sum(ar1b[...], axis=0) / total_obs + EPSILON)
    scale = ratio / beta
    squares = jnp.zeros((1, 128), F32)
    for l in range(8):
        own = scale * grad[l * 8 : l * 8 + 5] - beta * sv_ref[:, l * 128 : (l + 1) * 128]
        sraw_out[:, l * 128 : (l + 1) * 128] = own
        squares = squares + jnp.sum(own * own, axis=0, keepdims=True)

    each(n_src, lambda d: src_arrival(d, lambda o: rs_recv.at[o, pl.ds(0, 6)], rss, rsr).wait_recv())
    gathered = jnp.sum(rs_recv[...], axis=0)
    for a in range(3):
        for sub in range(2):
            row = a * 2 + sub
            own = scale * gathered[row : row + 1] - beta * kv_ref[a, :, sub * 128 : (sub + 1) * 128]
            kraw_out[a, :, sub * 128 : (sub + 1) * 128] = own
            squares = squares + own * own

    ar2a[s] = jnp.broadcast_to(jnp.sum(squares, axis=1, keepdims=True), (1, 128))
    each(n_src, lambda d: src_copy(d, lambda o: ar2a.at[s], ar2a.at[s], ar2as, ar2ar).start())
    each(n_src, lambda d: src_arrival(d, lambda o: ar2a.at[o], ar2as, ar2ar).wait_recv())
    ar2b[m] = jnp.sum(ar2a[...], axis=0)
    each(n_tm, lambda d: tm_copy(d, lambda o: ar2b.at[m], ar2b.at[m], ar2bs, ar2br).start())
    each(n_tm, lambda d: tm_arrival(d, lambda o: ar2b.at[o], ar2bs, ar2br).wait_recv())
    alpha_next = jnp.sqrt(jnp.sum(ar2b[...], axis=0) / unknowns + EPSILON)
    scal_out[0:1, :] = alpha_next
    scal_out[1:2, :] = beta

    each(n_src, lambda d: src_copy(d, lambda o: ag.at[s, pl.ds(0, 6)], ag.at[s, pl.ds(0, 6)], agss, agr).wait_send())
    each(n_tm, lambda d: tm_copy(d, lambda o: pbuf.at[o], prcv.at[m], prs, prr).wait_send())
    each(n_tm, lambda d: tm_copy(d, lambda o: rbuf.at[o], rrcv.at[m], rrs, rrr).wait_send())
    each(n_src, lambda d: src_copy(d, lambda o: ar1a.at[s], ar1a.at[s], ar1as, ar1ar).wait_send())
    each(n_src, lambda d: src_copy(d, lambda o: rs_send.at[o, pl.ds(0, 6)], rs_recv.at[s, pl.ds(0, 6)], rss, rsr).wait_send())
    each(n_tm, lambda d: tm_copy(d, lambda o: ar1b.at[m], ar1b.at[m], ar1bs, ar1br).wait_send())
    each(n_src, lambda d: src_copy(d, lambda o: ar2a.at[s], ar2a.at[s], ar2as, ar2ar).wait_send())
    each(n_tm, lambda d: tm_copy(d, lambda o: ar2b.at[m], ar2b.at[m], ar2bs, ar2br).wait_send())


def finish(
    raw_ref,
    sraw_ref,
    kraw_ref,
    scal_ref,
    ss_ref,
    ks_ref,
    sx_ref,
    kx_ref,
    rec_ref,
    left_out,
    snext_out,
    knext_out,
    ssearch_out,
    ksearch_out,
    sx_out,
    kx_out,
    rec_out,
):
    alpha_next = scal_ref[0:1, 0:1]
    beta = scal_ref[1:2, 0:1]
    pivot = rec_ref[1]
    remainder = rec_ref[2]
    radius = jnp.sqrt(pivot * pivot + beta * beta)
    cosine = pivot / radius
    sine = beta / radius
    coupling = sine * alpha_next
    gain = cosine * remainder / radius
    share = coupling / radius
    left_out[...] = raw_ref[...] / beta
    snext = sraw_ref[...] / alpha_next
    snext_out[...] = snext
    ssearch_out[...] = snext - share * ss_ref[...]
    sx_out[...] = sx_ref[...] + gain * ss_ref[...]
    for a in range(3):
        knext = kraw_ref[a] / alpha_next
        knext_out[a] = knext
        ksearch_out[a] = knext - share * ks_ref[a]
        kx_out[a] = kx_ref[a] + gain * ks_ref[a]
    lane = lax.broadcasted_iota(jnp.int32, (1, 4), 1)
    rec_out[...] = jnp.where(
        lane == 0,
        alpha_next,
        jnp.where(lane == 1, beta, jnp.where(lane == 2, -cosine * alpha_next, sine * remainder)),
    )


def shards(
    left_vector,
    source_coeffs,
    knot_coeffs,
    source_index,
    band_start,
    bucket_fill,
    source_vector,
    knot_vector,
    source_search,
    knot_search,
    source_solution,
    knot_solution,
    recurrence,
):
    n_tm = lax.axis_size("tm")
    n_src = lax.axis_size("src")
    devices = n_tm * n_src
    buckets, cap = left_vector.shape
    source_dev = source_vector.shape[1]
    knot_dev = knot_vector.shape[2]
    total_obs = buckets * cap * devices
    unknowns = (5 * source_dev + 3 * knot_dev) * devices
    vmem = pl.BlockSpec(memory_space=pltpu.VMEM)
    smem = pl.BlockSpec(memory_space=pltpu.SMEM)
    sem = pltpu.SemaphoreType.DMA
    sem_sizes = [n_src, n_tm, n_tm, n_src, n_src, n_tm, n_src, n_tm]
    raw, sraw, kraw, scal = pl.pallas_call(
        functools.partial(iterate, n_src, n_tm, total_obs, unknowns),
        out_shape=(
            jax.ShapeDtypeStruct((buckets, cap), F32),
            jax.ShapeDtypeStruct((5, source_dev), F32),
            jax.ShapeDtypeStruct((3, 1, knot_dev), F32),
            jax.ShapeDtypeStruct((2, 128), F32),
        ),
        in_specs=[vmem] * 8 + [smem],
        out_specs=[vmem] * 4,
        scratch_shapes=[
            pltpu.VMEM((n_src, 8, 128), F32),
            pltpu.VMEM((n_tm, 2, cap), F32),
            pltpu.VMEM((n_tm, 2, cap), F32),
            pltpu.VMEM((n_tm, 1, cap), F32),
            pltpu.VMEM((n_tm, 1, cap), F32),
            pltpu.VMEM((n_src, 8, 128), F32),
            pltpu.VMEM((n_src, 8, 128), F32),
            pltpu.VMEM((n_src, 1, 128), F32),
            pltpu.VMEM((n_tm, 1, 128), F32),
            pltpu.VMEM((n_src, 1, 128), F32),
            pltpu.VMEM((n_tm, 1, 128), F32),
            pltpu.VMEM((n_tm, 128, cap), BF16),
            pltpu.VMEM((n_tm, 128, cap), BF16),
            pltpu.VMEM((384, 128), F32),
            pltpu.VMEM((8, 128), F32),
            pltpu.SemaphoreType.DMA,
        ]
        + [sem((n,)) for n in sem_sizes]
        + [sem((n,)) for n in sem_sizes],
        compiler_params=pltpu.CompilerParams(collective_id=0, has_side_effects=True),
    )(
        left_vector,
        source_coeffs,
        knot_coeffs,
        source_index,
        band_start,
        bucket_fill,
        source_vector,
        knot_vector,
        recurrence,
    )
    outs = pl.pallas_call(
        finish,
        out_shape=(
            jax.ShapeDtypeStruct((buckets, cap), F32),
            jax.ShapeDtypeStruct((5, source_dev), F32),
            jax.ShapeDtypeStruct((3, 1, knot_dev), F32),
            jax.ShapeDtypeStruct((5, source_dev), F32),
            jax.ShapeDtypeStruct((3, 1, knot_dev), F32),
            jax.ShapeDtypeStruct((5, source_dev), F32),
            jax.ShapeDtypeStruct((3, 1, knot_dev), F32),
            jax.ShapeDtypeStruct((1, 4), F32),
        ),
        in_specs=[vmem] * 8 + [smem],
        out_specs=[vmem] * 8,
    )(raw, sraw, kraw, scal, source_search, knot_search, source_solution, knot_solution, recurrence)
    return (*outs[:7], outs[7].reshape(4))


def solution(mesh):
    in_specs = (
        P(None, ("src", "tm")),
        P(None, None, ("src", "tm")),
        P(None, None, ("src", "tm")),
        P(None, ("src", "tm")),
        P(None, ("src", "tm")),
        P(None, ("src", "tm")),
        P(None, ("src", "tm")),
        P(None, "tm", "src"),
        P(None, ("src", "tm")),
        P(None, "tm", "src"),
        P(None, ("src", "tm")),
        P(None, "tm", "src"),
        P(),
    )
    out_specs = (
        P(None, ("src", "tm")),
        P(None, ("src", "tm")),
        P(None, "tm", "src"),
        P(None, ("src", "tm")),
        P(None, "tm", "src"),
        P(None, ("src", "tm")),
        P(None, "tm", "src"),
        P(),
    )
    return jax.shard_map(shards, mesh=mesh, in_specs=in_specs, out_specs=out_specs, check_vma=False)
```

```python
import functools

import jax
import jax.numpy as jnp
from jax import lax
from jax.experimental import pallas as pl
from jax.experimental.pallas import tpu as pltpu
from jax.sharding import PartitionSpec as P

N_X = 4
EPSILON = 1e-06
F32 = jnp.float32
BF16 = jnp.bfloat16
NT = (((1,), (1,)), ((), ()))
NN = (((1,), (0,)), ((), ()))


def split3(x):
    hi = x.astype(BF16)
    rest = x - hi.astype(F32)
    mid = rest.astype(BF16)
    low = (rest - mid.astype(F32)).astype(BF16)
    return hi, mid, low


def split3_f32(x):
    return [part.astype(F32) for part in split3(x)]


def iterate(
    n_src,
    n_tm,
    total_obs,
    unknowns,
    left_hbm,
    sc_hbm,
    kc_hbm,
    si_hbm,
    bs_hbm,
    sv_hbm,
    kv_hbm,
    fill_ref,
    rec_ref,
    raw_out,
    sraw_out,
    kraw_out,
    scal_out,
    left_ref,
    sc_ref,
    kc_ref,
    si_ref,
    bs_ref,
    sv_ref,
    kv_ref,
    ag,
    pbuf,
    prcv,
    rbuf,
    rrcv,
    rs_send,
    rs_recv,
    ar1a,
    ar1b,
    ar2a,
    ar2b,
    ohs,
    ohk,
    acc,
    load_sem,
    ag_sem,
    p_sem,
    r_sem,
    rs_sem,
    ar1a_sem,
    ar1b_sem,
    ar2a_sem,
    ar2b_sem,
):
    s = lax.axis_index("src")
    m = lax.axis_index("tm")
    ratio = unknowns / total_obs
    cap = left_ref.shape[1]
    n_z = n_src // N_X
    z = lax.div(s, N_X)
    x = lax.rem(s, N_X)
    pending = []

    src_order = [n_src // 2] + [sign * d for d in range(n_src // 2 - 1, 0, -1) for sign in (1, -1)]
    tm_order = list(range(1, n_tm))

    def send_all(axis, order, me, n, src, dst, sems):
        for d in order:
            o = lax.rem(me + d + n, n)
            pltpu.make_async_remote_copy(
                src_ref=src(o),
                dst_ref=dst,
                send_sem=sems.at[0],
                recv_sem=sems.at[1],
                device_id={axis: o},
                device_id_type=pl.DeviceIdType.MESH,
            ).start()

    def arrived(axis, whole, sems, which):
        copy = pltpu.make_async_remote_copy(
            src_ref=whole,
            dst_ref=whole,
            send_sem=sems.at[0],
            recv_sem=sems.at[1],
            device_id={axis: 0},
            device_id_type=pl.DeviceIdType.MESH,
        )
        return copy.wait_recv() if which else copy.wait_send()

    def src_send(src, dst, whole, sems):
        send_all("src", src_order, s, n_src, src, dst, sems)
        pending.append(lambda: arrived("src", whole, sems, 0))

    def tm_send(src, dst, whole, sems):
        send_all("tm", tm_order, m, n_tm, src, dst, sems)
        pending.append(lambda: arrived("tm", whole, sems, 0))

    src_rest = pl.ds(0, n_src - 1)
    tm_rest = pl.ds(0, n_tm - 1)
    six = pl.ds(0, 6)

    def at(dz, dx):
        return lax.rem(z + dz + n_z, n_z) * N_X + lax.rem(x + dx, N_X)

    near = [(dz, dx) for dz in (4, -4, 3, -3, 2, -2, 1, -1, 0) for dx in (2, 1, 3, 0) if dz or dx]

    barrier = pltpu.get_barrier_semaphore()
    for dz, dx in near:
        pl.semaphore_signal(barrier, inc=1, device_id={"src": at(dz, dx)}, device_id_type=pl.DeviceIdType.MESH)
    for d in tm_order:
        pl.semaphore_signal(
            barrier, inc=1, device_id={"tm": lax.rem(m + d, n_tm)}, device_id_type=pl.DeviceIdType.MESH
        )

    loads = [
        pltpu.make_async_copy(src, dst, load_sem.at[n])
        for n, (src, dst) in enumerate(
            (
                (kv_hbm, kv_ref),
                (sv_hbm, sv_ref),
                (si_hbm, si_ref),
                (sc_hbm, sc_ref),
                (left_hbm, left_ref),
                (bs_hbm, bs_ref),
                (kc_hbm, kc_ref),
            )
        )
    ]
    for load in loads:
        load.start()
    for load in loads[:5]:
        load.wait()

    for a in range(3):
        for sub in range(2):
            ag[s, a * 2 + sub : a * 2 + sub + 1, :] = kv_ref[a, :, sub * 128 : (sub + 1) * 128]

    alpha = rec_ref[0]
    pad3 = jnp.zeros((3, 128), F32)
    table = jnp.concatenate(
        [jnp.concatenate([sv_ref[:, l * 128 : (l + 1) * 128], pad3], axis=0) for l in range(8)], axis=0
    )
    stable = jnp.concatenate(split3(table), axis=1)
    rows128 = lax.broadcasted_iota(jnp.int32, (128, cap), 0)
    lane = lax.broadcasted_iota(jnp.int32, (1, cap), 1)

    for t in range(n_tm):
        idx = si_ref[t : t + 1, :]
        hi = jnp.bitwise_and(idx, 127)
        lo = jnp.right_shift(idx, 7)
        oh = jnp.where(rows128 == hi, 1.0, 0.0).astype(BF16)
        ohs[t] = oh
        found = lax.dot_general(
            stable, jnp.concatenate([oh, oh, oh], axis=0), NN, preferred_element_type=F32
        )
        picked = jnp.zeros((8, cap), F32)
        for l in range(8):
            picked = picked + jnp.where(lo == l, found[l * 8 : (l + 1) * 8], 0.0)
        coef = sc_ref[:, t, :]
        image = jnp.sum(coef * picked[0:5], axis=0, keepdims=True)
        pbuf[t, 0:1, :] = image - alpha * left_ref[t : t + 1, :]
        pbuf[t, 1:2, :] = jnp.where(lane < fill_ref[t], 1.0, 0.0)

    pl.semaphore_wait(barrier, len(near) + n_tm - 1)

    def hand_on(block, target, which):
        pltpu.make_async_remote_copy(
            src_ref=block,
            dst_ref=block,
            send_sem=ag_sem.at[0],
            recv_sem=ag_sem.at[which],
            device_id={"src": target},
            device_id_type=pl.DeviceIdType.MESH,
        ).start()

    def taken(blocks, which):
        whole = ag.at[pl.ds(0, blocks), six]
        copy = pltpu.make_async_remote_copy(
            src_ref=whole,
            dst_ref=whole,
            send_sem=ag_sem.at[0],
            recv_sem=ag_sem.at[which],
            device_id={"src": s},
            device_id_type=pl.DeviceIdType.MESH,
        )
        return copy.wait_recv() if which else copy.wait_send()

    for dz, dx in near:
        hand_on(ag.at[s, six], at(dz, dx), 1 if dz == 4 else 2 if dz == -4 else 3)
    pending.append(lambda: taken(n_src - 1, 0))
    tm_send(lambda o: pbuf.at[o], prcv.at[m], pbuf.at[tm_rest], p_sem)
    prcv[m] = pbuf[m]
    for which, sign, reach in ((1, 1, 4), (2, -1, 3)):
        taken(N_X, which)
        plane = ag.at[pl.ds(lax.rem(z - sign * 4 + n_z, n_z) * N_X, N_X), six]
        for k in range(reach, 0, -1):
            hand_on(plane, at(sign * k, 0), 4)

    for load in loads[5:]:
        load.wait()

    for i in range(n_tm):
        band = bs_ref[i : i + 1, :]
        hi = jnp.bitwise_and(jnp.right_shift(band, 5), 1) * 64 + jnp.right_shift(band, 6)
        ohk[i] = jnp.where(rows128 == hi, 1.0, 0.0).astype(BF16)

    arrived("tm", prcv.at[tm_rest], p_sem, 1)
    taken(len(near) - 2 * N_X, 3)
    taken(7 * N_X, 4)

    parts = []
    for a in range(3):
        whole = jnp.concatenate([ag[:, a * 2 + sub, :] for sub in range(2)], axis=0)
        parts.append(jnp.concatenate(split3(jnp.transpose(whole)), axis=1))
    ktable = jnp.concatenate(parts, axis=0)

    band_rows = jnp.right_shift(rows128, 2)
    total = jnp.zeros((1, cap), F32)
    acc[...] = jnp.zeros_like(acc)
    for i in range(n_tm):
        oh = ohk[i]
        found = lax.dot_general(
            ktable, jnp.concatenate([oh, oh, oh], axis=0), NN, preferred_element_type=F32
        )
        lo = jnp.bitwise_and(bs_ref[i : i + 1, :], 31)
        hit = band_rows == lo
        coefs = []
        mixed = None
        for a in range(3):
            four = kc_ref[a * 4 : a * 4 + 4, i, :]
            eight = jnp.concatenate([four, four], axis=0)
            coefs.append(eight)
            term = found[a * 128 : (a + 1) * 128].reshape(16, 8, cap) * eight[None]
            mixed = term if mixed is None else mixed + term
        image = jnp.sum(jnp.where(hit, mixed.reshape(128, cap), 0.0), axis=0, keepdims=True)
        raw = prcv[i, 1:2, :] * (prcv[i, 0:1, :] + image)
        rbuf[i] = raw
        total = total + raw * raw
        hit_b = jnp.where(hit, 1.0, 0.0).astype(BF16)
        spread = [[], [], []]
        for a in range(3):
            for q, part in enumerate(split3_f32(coefs[a] * raw)):
                two = jnp.concatenate([part, part], axis=0).astype(BF16)
                spread[q].append(hit_b * jnp.concatenate([two] * 8, axis=0))
        terms = jnp.concatenate([jnp.concatenate(rows, axis=0) for rows in spread], axis=1)
        acc[...] += lax.dot_general(
            terms, jnp.concatenate([oh, oh, oh], axis=1), NT, preferred_element_type=F32
        )

    ar1a[s] = jnp.broadcast_to(jnp.sum(total, axis=1, keepdims=True), (1, 128))
    tm_send(lambda o: rbuf.at[o], rrcv.at[m], rbuf.at[tm_rest], r_sem)
    rrcv[m] = rbuf[m]
    src_send(lambda o: ar1a.at[s], ar1a.at[s], ar1a.at[src_rest], ar1a_sem)
    for a in range(3):
        turned = jnp.transpose(acc[a * 128 : (a + 1) * 128, :])
        for sub in range(2):
            rs_send[:, a * 2 + sub, :] = turned[sub * 64 : (sub + 1) * 64]

    src_send(lambda o: rs_send.at[o, six], rs_recv.at[s, six], rs_send.at[src_rest, six], rs_sem)
    rs_recv[s] = rs_send[s]

    arrived("tm", rrcv.at[tm_rest], r_sem, 1)
    grad = jnp.zeros((64, 128), F32)
    for t in range(n_tm):
        raw = rrcv[t]
        raw_out[t : t + 1, :] = raw
        lo = jnp.right_shift(si_ref[t : t + 1, :], 7)
        coef = jnp.concatenate([sc_ref[:, t, :], jnp.zeros((3, cap), F32)], axis=0)
        spread = []
        for part in split3_f32(coef * raw):
            spread.append(
                jnp.concatenate([jnp.where(lo == l, part, 0.0) for l in range(8)], axis=0).astype(BF16)
            )
        oh = ohs[t]
        grad = grad + lax.dot_general(
            jnp.concatenate(spread, axis=1),
            jnp.concatenate([oh, oh, oh], axis=1),
            NT,
            preferred_element_type=F32,
        )

    arrived("src", ar1a.at[src_rest], ar1a_sem, 1)
    ar1b[m] = jnp.sum(ar1a[...], axis=0)
    tm_send(lambda o: ar1b.at[m], ar1b.at[m], ar1b.at[tm_rest], ar1b_sem)
    arrived("tm", ar1b.at[tm_rest], ar1b_sem, 1)
    beta = jnp.sqrt(jnp.sum(ar1b[...], axis=0) / total_obs + EPSILON)
    scale = ratio / beta
    squares = jnp.zeros((1, 128), F32)
    for l in range(8):
        own = scale * grad[l * 8 : l * 8 + 5] - beta * sv_ref[:, l * 128 : (l + 1) * 128]
        sraw_out[:, l * 128 : (l + 1) * 128] = own
        squares = squares + jnp.sum(own * own, axis=0, keepdims=True)

    arrived("src", rs_recv.at[src_rest, six], rs_sem, 1)
    gathered = jnp.sum(rs_recv[...], axis=0)
    for a in range(3):
        for sub in range(2):
            row = a * 2 + sub
            own = scale * gathered[row : row + 1] - beta * kv_ref[a, :, sub * 128 : (sub + 1) * 128]
            kraw_out[a, :, sub * 128 : (sub + 1) * 128] = own
            squares = squares + own * own

    ar2a[s] = jnp.broadcast_to(jnp.sum(squares, axis=1, keepdims=True), (1, 128))
    src_send(lambda o: ar2a.at[s], ar2a.at[s], ar2a.at[src_rest], ar2a_sem)
    arrived("src", ar2a.at[src_rest], ar2a_sem, 1)
    ar2b[m] = jnp.sum(ar2a[...], axis=0)
    tm_send(lambda o: ar2b.at[m], ar2b.at[m], ar2b.at[tm_rest], ar2b_sem)
    arrived("tm", ar2b.at[tm_rest], ar2b_sem, 1)
    alpha_next = jnp.sqrt(jnp.sum(ar2b[...], axis=0) / unknowns + EPSILON)
    scal_out[0:1, :] = alpha_next
    scal_out[1:2, :] = beta

    for wait in pending:
        wait()


def finish(
    raw_ref,
    sraw_ref,
    kraw_ref,
    scal_ref,
    ss_ref,
    ks_ref,
    sx_ref,
    kx_ref,
    rec_ref,
    left_out,
    snext_out,
    knext_out,
    ssearch_out,
    ksearch_out,
    sx_out,
    kx_out,
    rec_out,
):
    alpha_next = scal_ref[0:1, 0:1]
    beta = scal_ref[1:2, 0:1]
    pivot = rec_ref[1]
    remainder = rec_ref[2]
    radius = jnp.sqrt(pivot * pivot + beta * beta)
    cosine = pivot / radius
    sine = beta / radius
    coupling = sine * alpha_next
    gain = cosine * remainder / radius
    share = coupling / radius
    left_out[...] = raw_ref[...] / beta
    snext = sraw_ref[...] / alpha_next
    snext_out[...] = snext
    ssearch_out[...] = snext - share * ss_ref[...]
    sx_out[...] = sx_ref[...] + gain * ss_ref[...]
    for a in range(3):
        knext = kraw_ref[a] / alpha_next
        knext_out[a] = knext
        ksearch_out[a] = knext - share * ks_ref[a]
        kx_out[a] = kx_ref[a] + gain * ks_ref[a]
    lane = lax.broadcasted_iota(jnp.int32, (1, 4), 1)
    rec_out[...] = jnp.where(
        lane == 0,
        alpha_next,
        jnp.where(lane == 1, beta, jnp.where(lane == 2, -cosine * alpha_next, sine * remainder)),
    )


def shards(
    left_vector,
    source_coeffs,
    knot_coeffs,
    source_index,
    band_start,
    bucket_fill,
    source_vector,
    knot_vector,
    source_search,
    knot_search,
    source_solution,
    knot_solution,
    recurrence,
):
    n_tm = lax.axis_size("tm")
    n_src = lax.axis_size("src")
    devices = n_tm * n_src
    buckets, cap = left_vector.shape
    source_dev = source_vector.shape[1]
    knot_dev = knot_vector.shape[2]
    total_obs = buckets * cap * devices
    unknowns = (5 * source_dev + 3 * knot_dev) * devices
    vmem = pl.BlockSpec(memory_space=pltpu.VMEM)
    smem = pl.BlockSpec(memory_space=pltpu.SMEM)
    hbm = pl.BlockSpec(memory_space=pl.ANY)
    raw, sraw, kraw, scal = pl.pallas_call(
        functools.partial(iterate, n_src, n_tm, total_obs, unknowns),
        out_shape=(
            jax.ShapeDtypeStruct((buckets, cap), F32),
            jax.ShapeDtypeStruct((5, source_dev), F32),
            jax.ShapeDtypeStruct((3, 1, knot_dev), F32),
            jax.ShapeDtypeStruct((2, 128), F32),
        ),
        in_specs=[hbm] * 7 + [smem] * 2,
        out_specs=[vmem] * 4,
        scratch_shapes=[
            pltpu.VMEM(a.shape, a.dtype)
            for a in (
                left_vector,
                source_coeffs,
                knot_coeffs,
                source_index,
                band_start,
                source_vector,
                knot_vector,
            )
        ]
        + [
            pltpu.VMEM((n_src, 8, 128), F32),
            pltpu.VMEM((n_tm, 2, cap), F32),
            pltpu.VMEM((n_tm, 2, cap), F32),
            pltpu.VMEM((n_tm, 1, cap), F32),
            pltpu.VMEM((n_tm, 1, cap), F32),
            pltpu.VMEM((n_src, 8, 128), F32),
            pltpu.VMEM((n_src, 8, 128), F32),
            pltpu.VMEM((n_src, 1, 128), F32),
            pltpu.VMEM((n_tm, 1, 128), F32),
            pltpu.VMEM((n_src, 1, 128), F32),
            pltpu.VMEM((n_tm, 1, 128), F32),
            pltpu.VMEM((n_tm, 128, cap), BF16),
            pltpu.VMEM((n_tm, 128, cap), BF16),
            pltpu.VMEM((384, 128), F32),
            pltpu.SemaphoreType.DMA((7,)),
        ]
        + [pltpu.SemaphoreType.DMA((5,))] + [pltpu.SemaphoreType.DMA((2,))] * 7,
        compiler_params=pltpu.CompilerParams(collective_id=0, has_side_effects=True),
    )(
        left_vector,
        source_coeffs,
        knot_coeffs,
        source_index,
        band_start,
        source_vector,
        knot_vector,
        bucket_fill.reshape(buckets),
        recurrence,
    )
    outs = pl.pallas_call(
        finish,
        out_shape=(
            jax.ShapeDtypeStruct((buckets, cap), F32),
            jax.ShapeDtypeStruct((5, source_dev), F32),
            jax.ShapeDtypeStruct((3, 1, knot_dev), F32),
            jax.ShapeDtypeStruct((5, source_dev), F32),
            jax.ShapeDtypeStruct((3, 1, knot_dev), F32),
            jax.ShapeDtypeStruct((5, source_dev), F32),
            jax.ShapeDtypeStruct((3, 1, knot_dev), F32),
            jax.ShapeDtypeStruct((1, 4), F32),
        ),
        in_specs=[vmem] * 8 + [smem],
        out_specs=[vmem] * 8,
    )(raw, sraw, kraw, scal, source_search, knot_search, source_solution, knot_solution, recurrence)
    return (*outs[:7], outs[7].reshape(4))


def solution(mesh):
    in_specs = (
        P(None, ("src", "tm")),
        P(None, None, ("src", "tm")),
        P(None, None, ("src", "tm")),
        P(None, ("src", "tm")),
        P(None, ("src", "tm")),
        P(None, ("src", "tm")),
        P(None, ("src", "tm")),
        P(None, "tm", "src"),
        P(None, ("src", "tm")),
        P(None, "tm", "src"),
        P(None, ("src", "tm")),
        P(None, "tm", "src"),
        P(),
    )
    out_specs = (
        P(None, ("src", "tm")),
        P(None, ("src", "tm")),
        P(None, "tm", "src"),
        P(None, ("src", "tm")),
        P(None, "tm", "src"),
        P(None, ("src", "tm")),
        P(None, "tm", "src"),
        P(),
    )
    return jax.shard_map(shards, mesh=mesh, in_specs=in_specs, out_specs=out_specs, check_vma=False)
```

```python
import functools

import jax
import jax.numpy as jnp
from jax import lax
from jax.experimental import pallas as pl
from jax.experimental.pallas import tpu as pltpu
from jax.sharding import PartitionSpec as P

N_X = 4
EPSILON = 1e-06
F32 = jnp.float32
BF16 = jnp.bfloat16
NT = (((1,), (1,)), ((), ()))
NN = (((1,), (0,)), ((), ()))


def split3(x):
    hi = x.astype(BF16)
    rest = x - hi.astype(F32)
    mid = rest.astype(BF16)
    low = (rest - mid.astype(F32)).astype(BF16)
    return hi, mid, low


def split3_f32(x):
    return [part.astype(F32) for part in split3(x)]


def iterate(
    n_src,
    n_tm,
    total_obs,
    unknowns,
    left_hbm,
    sc_hbm,
    kc_hbm,
    si_hbm,
    bs_hbm,
    sv_hbm,
    kv_hbm,
    fill_hbm,
    rec_hbm,
    ss_hbm,
    ks_hbm,
    sx_hbm,
    kx_hbm,
    raw_out,
    sraw_out,
    kraw_out,
    scal_out,
    ss_out,
    ks_out,
    sx_out,
    kx_out,
    left_ref,
    sc_ref,
    kc_ref,
    si_ref,
    bs_ref,
    sv_ref,
    kv_ref,
    fill_ref,
    rec_ref,
    ag,
    pbuf,
    prcv,
    rbuf,
    rrcv,
    rs_send,
    rs_recv,
    ar1a,
    ar1b,
    ar2a,
    ar2b,
    ohs,
    ohk,
    cl,
    load_sem,
    ag_sem,
    p_sem,
    r_sem,
    rs_sem,
    ar1a_sem,
    ar1b_sem,
    ar2a_sem,
    ar2b_sem,
):
    s = lax.axis_index("src")
    m = lax.axis_index("tm")
    ratio = unknowns / total_obs
    cap = left_ref.shape[1]
    n_z = n_src // N_X
    z = lax.div(s, N_X)
    x = lax.rem(s, N_X)
    pending = []

    src_order = [n_src // 2] + [sign * d for d in range(n_src // 2 - 1, 0, -1) for sign in (1, -1)]
    tm_order = list(range(1, n_tm))

    def send_all(axis, order, me, n, src, dst, sems):
        for d in order:
            o = lax.rem(me + d + n, n)
            pltpu.make_async_remote_copy(
                src_ref=src(o),
                dst_ref=dst,
                send_sem=sems.at[0],
                recv_sem=sems.at[1],
                device_id={axis: o},
                device_id_type=pl.DeviceIdType.MESH,
            ).start()

    def arrived(axis, whole, sems, which):
        copy = pltpu.make_async_remote_copy(
            src_ref=whole,
            dst_ref=whole,
            send_sem=sems.at[0],
            recv_sem=sems.at[1],
            device_id={axis: 0},
            device_id_type=pl.DeviceIdType.MESH,
        )
        return copy.wait_recv() if which else copy.wait_send()

    def src_send(src, dst, whole, sems):
        send_all("src", src_order, s, n_src, src, dst, sems)
        pending.append(lambda: arrived("src", whole, sems, 0))

    def tm_send(src, dst, whole, sems):
        send_all("tm", tm_order, m, n_tm, src, dst, sems)
        pending.append(lambda: arrived("tm", whole, sems, 0))

    src_rest = pl.ds(0, n_src - 1)
    tm_rest = pl.ds(0, n_tm - 1)
    six = pl.ds(0, 6)

    def at(dz, dx):
        return lax.rem(z + dz + n_z, n_z) * N_X + lax.rem(x + dx, N_X)

    near = [(dz, dx) for dz in (4, -4, 3, -3, 2, -2, 1, -1, 0) for dx in (2, 1, 3, 0) if dz or dx]

    loads = [
        pltpu.make_async_copy(src, dst, load_sem.at[n])
        for n, (src, dst) in enumerate(
            (
                (kv_hbm, kv_ref),
                (rec_hbm, rec_ref),
                (fill_hbm, fill_ref),
                (sv_hbm, sv_ref),
                (si_hbm, si_ref),
                (sc_hbm, sc_ref),
                (left_hbm, left_ref),
                (bs_hbm, bs_ref),
                (kc_hbm, kc_ref),
                (ss_hbm, ss_out),
                (ks_hbm, ks_out),
                (sx_hbm, sx_out),
                (kx_hbm, kx_out),
            )
        )
    ]
    for load in loads:
        load.start()

    barrier = pltpu.get_barrier_semaphore()
    for dz, dx in near:
        pl.semaphore_signal(barrier, inc=1, device_id={"src": at(dz, dx)}, device_id_type=pl.DeviceIdType.MESH)
    for d in tm_order:
        pl.semaphore_signal(
            barrier, inc=1, device_id={"tm": lax.rem(m + d, n_tm)}, device_id_type=pl.DeviceIdType.MESH
        )

    for load in loads[:7]:
        load.wait()

    for a in range(3):
        for sub in range(2):
            ag[s, a * 2 + sub : a * 2 + sub + 1, :] = kv_ref[a, :, sub * 128 : (sub + 1) * 128]

    alpha = rec_ref[0]
    pad3 = jnp.zeros((3, 128), F32)
    table = jnp.concatenate(
        [jnp.concatenate([sv_ref[:, l * 128 : (l + 1) * 128], pad3], axis=0) for l in range(8)], axis=0
    )
    stable = jnp.concatenate(split3(table), axis=1)
    rows128 = lax.broadcasted_iota(jnp.int32, (128, cap), 0)
    lane = lax.broadcasted_iota(jnp.int32, (1, cap), 1)

    for t in range(n_tm):
        idx = si_ref[t : t + 1, :]
        hi = jnp.bitwise_and(idx, 127)
        lo = jnp.right_shift(idx, 7)
        oh = jnp.where(rows128 == hi, 1.0, 0.0).astype(BF16)
        ohs[t] = oh
        found = lax.dot_general(
            stable, jnp.concatenate([oh, oh, oh], axis=0), NN, preferred_element_type=F32
        )
        picked = jnp.zeros((8, cap), F32)
        for l in range(8):
            picked = picked + jnp.where(lo == l, found[l * 8 : (l + 1) * 8], 0.0)
        coef = sc_ref[:, t, :]
        image = jnp.sum(coef * picked[0:5], axis=0, keepdims=True)
        pbuf[t, 0:1, :] = image - alpha * left_ref[t : t + 1, :]
        pbuf[t, 1:2, :] = jnp.where(lane < fill_ref[t], 1.0, 0.0)

    pl.semaphore_wait(barrier, len(near) + n_tm - 1)

    def hand_on(block, target, which):
        pltpu.make_async_remote_copy(
            src_ref=block,
            dst_ref=block,
            send_sem=ag_sem.at[0],
            recv_sem=ag_sem.at[which],
            device_id={"src": target},
            device_id_type=pl.DeviceIdType.MESH,
        ).start()

    def taken(blocks, which):
        whole = ag.at[pl.ds(0, blocks), six]
        copy = pltpu.make_async_remote_copy(
            src_ref=whole,
            dst_ref=whole,
            send_sem=ag_sem.at[0],
            recv_sem=ag_sem.at[which],
            device_id={"src": s},
            device_id_type=pl.DeviceIdType.MESH,
        )
        return copy.wait_recv() if which else copy.wait_send()

    for dz, dx in near:
        hand_on(ag.at[s, six], at(dz, dx), 1 if dz == 4 else 2 if dz == -4 else 3)
    pending.append(lambda: taken(n_src - 1, 0))
    tm_send(lambda o: pbuf.at[o], prcv.at[m], pbuf.at[tm_rest], p_sem)
    prcv[m] = pbuf[m]
    for which, sign, reach in ((1, 1, 4), (2, -1, 3)):
        taken(N_X, which)
        plane = ag.at[pl.ds(lax.rem(z - sign * 4 + n_z, n_z) * N_X, N_X), six]
        for k in range(reach, 0, -1):
            hand_on(plane, at(sign * k, 0), 4)

    for load in loads[7:]:
        load.wait()

    rows256 = lax.broadcasted_iota(jnp.int32, (256, cap), 0)
    for i in range(n_tm):
        band = bs_ref[i : i + 1, :]
        hi = (
            jnp.bitwise_and(jnp.right_shift(band, 4), 1) * 128
            + jnp.bitwise_and(jnp.right_shift(band, 5), 1) * 64
            + jnp.right_shift(band, 6)
        )
        ohk[i] = jnp.where(rows256 == hi, 1.0, 0.0).astype(BF16)

    arrived("tm", prcv.at[tm_rest], p_sem, 1)
    taken(len(near) - 2 * N_X, 3)
    taken(7 * N_X, 4)

    table = []
    for a in range(3):
        whole = jnp.concatenate([ag[:, a * 2 + half, :] for half in range(2)], axis=0)
        turned = jnp.transpose(whole)
        table.append(jnp.concatenate([turned[0:64], turned[64:128]], axis=1))
    ktable = jnp.concatenate(split3(jnp.concatenate(table, axis=0)), axis=0)

    band_rows = jnp.right_shift(lax.broadcasted_iota(jnp.int32, (64, cap), 0), 2)
    total = jnp.zeros((1, cap), F32)
    for i in range(n_tm):
        three = lax.dot_general(ktable, ohk[i], NN, preferred_element_type=F32)
        found = three[0:192] + three[192:384] + three[384:576]
        lo = jnp.bitwise_and(bs_ref[i : i + 1, :], 15)
        coefs = []
        mixed = None
        for a in range(3):
            four = kc_ref[a * 4 : a * 4 + 4, i, :]
            eight = jnp.concatenate([four, four], axis=0)
            coefs.append(eight)
            term = found[a * 64 : (a + 1) * 64].reshape(8, 8, cap) * eight[None]
            mixed = term if mixed is None else mixed + term
        image = jnp.sum(jnp.where(band_rows == lo, mixed.reshape(64, cap), 0.0), axis=0, keepdims=True)
        raw = prcv[i, 1:2, :] * (prcv[i, 0:1, :] + image)
        rbuf[i] = raw
        total = total + raw * raw
        for a in range(3):
            for q, part in enumerate(split3_f32(coefs[a] * raw)):
                cl[i, q * 3 + a] = jnp.concatenate([part, part], axis=0).astype(BF16)
    ar1a[s] = total[:, 0:128] + total[:, 128:256]
    src_send(lambda o: ar1a.at[s], ar1a.at[s], ar1a.at[src_rest], ar1a_sem)
    tm_send(lambda o: rbuf.at[o], rrcv.at[m], rbuf.at[tm_rest], r_sem)
    rrcv[m] = rbuf[m]

    acc = jnp.zeros((192, 256), F32)
    for i in range(n_tm):
        lo = jnp.bitwise_and(bs_ref[i : i + 1, :], 15)
        hit = jnp.where(band_rows == lo, 1.0, 0.0).astype(BF16)
        terms = jnp.concatenate(
            [hit * jnp.concatenate([cl[i, row]] * 4, axis=0) for row in range(9)], axis=0
        )
        three = lax.dot_general(terms, ohk[i], NT, preferred_element_type=F32)
        acc = acc + (three[0:192] + three[192:384] + three[384:576])
    for a in range(3):
        own = acc[a * 64 : (a + 1) * 64]
        turned = jnp.transpose(jnp.concatenate([own[:, 0:128], own[:, 128:256]], axis=0))
        for half in range(2):
            rs_send[:, a * 2 + half, :] = turned[half * 64 : (half + 1) * 64]

    src_send(lambda o: rs_send.at[o, six], rs_recv.at[s, six], rs_send.at[src_rest, six], rs_sem)
    rs_recv[s] = rs_send[s]
    arrived("tm", rrcv.at[tm_rest], r_sem, 1)

    grad = jnp.zeros((64, 128), F32)
    for t in range(n_tm):
        raw = rrcv[t]
        raw_out[t : t + 1, :] = raw
        lo = jnp.right_shift(si_ref[t : t + 1, :], 7)
        coef = jnp.concatenate([sc_ref[:, t, :], jnp.zeros((3, cap), F32)], axis=0)
        spread = []
        for part in split3_f32(coef * raw):
            spread.append(
                jnp.concatenate([jnp.where(lo == l, part, 0.0) for l in range(8)], axis=0).astype(BF16)
            )
        oh = ohs[t]
        grad = grad + lax.dot_general(
            jnp.concatenate(spread, axis=1),
            jnp.concatenate([oh, oh, oh], axis=1),
            NT,
            preferred_element_type=F32,
        )

    arrived("src", ar1a.at[src_rest], ar1a_sem, 1)
    ar1b[m] = jnp.sum(ar1a[...], axis=0)
    tm_send(lambda o: ar1b.at[m], ar1b.at[m], ar1b.at[tm_rest], ar1b_sem)
    arrived("tm", ar1b.at[tm_rest], ar1b_sem, 1)
    beta = jnp.sqrt(jnp.sum(jnp.sum(ar1b[...], axis=0), axis=1, keepdims=True) / total_obs + EPSILON)
    scale = ratio / beta
    squares = jnp.zeros((1, 128), F32)
    for l in range(8):
        own = scale * grad[l * 8 : l * 8 + 5] - beta * sv_ref[:, l * 128 : (l + 1) * 128]
        sraw_out[:, l * 128 : (l + 1) * 128] = own
        squares = squares + jnp.sum(own * own, axis=0, keepdims=True)

    arrived("src", rs_recv.at[src_rest, six], rs_sem, 1)
    gathered = jnp.sum(rs_recv[...], axis=0)
    for a in range(3):
        for sub in range(2):
            row = a * 2 + sub
            own = scale * gathered[row : row + 1] - beta * kv_ref[a, :, sub * 128 : (sub + 1) * 128]
            kraw_out[a, :, sub * 128 : (sub + 1) * 128] = own
            squares = squares + own * own

    ar2b[m] = squares
    tm_send(lambda o: ar2b.at[m], ar2b.at[m], ar2b.at[tm_rest], ar2b_sem)
    arrived("tm", ar2b.at[tm_rest], ar2b_sem, 1)
    ar2a[s] = jnp.sum(ar2b[...], axis=0)
    src_send(lambda o: ar2a.at[s], ar2a.at[s], ar2a.at[src_rest], ar2a_sem)
    arrived("src", ar2a.at[src_rest], ar2a_sem, 1)
    alpha_next = jnp.sqrt(
        jnp.sum(jnp.sum(ar2a[...], axis=0), axis=1, keepdims=True) / unknowns + EPSILON
    )
    pivot = rec_ref[1]
    remainder = rec_ref[2]
    radius = jnp.sqrt(pivot * pivot + beta * beta)
    cosine = pivot / radius
    sine = beta / radius
    wide = (1, 128)
    lane = lax.broadcasted_iota(jnp.int32, wide, 1)
    scal_out[0:1, :] = jnp.broadcast_to(alpha_next, wide)
    scal_out[1:2, :] = jnp.broadcast_to(beta, wide)
    scal_out[2:3, :] = jnp.broadcast_to(cosine * remainder / radius, wide)
    scal_out[3:4, :] = jnp.broadcast_to(sine * alpha_next / radius, wide)
    scal_out[4:5, :] = jnp.where(
        lane == 0,
        alpha_next,
        jnp.where(lane == 1, beta, jnp.where(lane == 2, -cosine * alpha_next, sine * remainder)),
    )
    for wait in pending:
        wait()


def finish(
    raw_ref,
    sraw_ref,
    kraw_ref,
    scal_ref,
    ss_ref,
    ks_ref,
    sx_ref,
    kx_ref,
    left_out,
    snext_out,
    knext_out,
    ssearch_out,
    ksearch_out,
    sx_out,
    kx_out,
    rec_out,
):
    alpha_next = scal_ref[0:1, 0:1]
    beta = scal_ref[1:2, 0:1]
    gain = scal_ref[2:3, 0:1]
    share = scal_ref[3:4, 0:1]
    left_out[...] = raw_ref[...] / beta
    snext = sraw_ref[...] / alpha_next
    snext_out[...] = snext
    ssearch_out[...] = snext - share * ss_ref[...]
    sx_out[...] = sx_ref[...] + gain * ss_ref[...]
    for a in range(3):
        knext = kraw_ref[a] / alpha_next
        knext_out[a] = knext
        ksearch_out[a] = knext - share * ks_ref[a]
        kx_out[a] = kx_ref[a] + gain * ks_ref[a]
    rec_out[...] = scal_ref[4:5, 0:4]


def shards(
    left_vector,
    source_coeffs,
    knot_coeffs,
    source_index,
    band_start,
    bucket_fill,
    source_vector,
    knot_vector,
    source_search,
    knot_search,
    source_solution,
    knot_solution,
    recurrence,
):
    n_tm = lax.axis_size("tm")
    n_src = lax.axis_size("src")
    devices = n_tm * n_src
    buckets, cap = left_vector.shape
    source_dev = source_vector.shape[1]
    knot_dev = knot_vector.shape[2]
    total_obs = buckets * cap * devices
    unknowns = (5 * source_dev + 3 * knot_dev) * devices
    vmem = pl.BlockSpec(memory_space=pltpu.VMEM)
    hbm = pl.BlockSpec(memory_space=pl.ANY)
    held = pl.pallas_call(
        functools.partial(iterate, n_src, n_tm, total_obs, unknowns),
        out_shape=(
            pltpu.VMEM((buckets, cap), F32),
            pltpu.VMEM((5, source_dev), F32),
            pltpu.VMEM((3, 1, knot_dev), F32),
            pltpu.VMEM((8, 128), F32),
            pltpu.VMEM((5, source_dev), F32),
            pltpu.VMEM((3, 1, knot_dev), F32),
            pltpu.VMEM((5, source_dev), F32),
            pltpu.VMEM((3, 1, knot_dev), F32),
        ),
        in_specs=[hbm] * 13,
        out_specs=[vmem] * 8,
        scratch_shapes=[
            pltpu.VMEM(a.shape, a.dtype)
            for a in (
                left_vector,
                source_coeffs,
                knot_coeffs,
                source_index,
                band_start,
                source_vector,
                knot_vector,
            )
        ]
        + [
            pltpu.SMEM((buckets,), jnp.int32),
            pltpu.SMEM((3,), F32),
            pltpu.VMEM((n_src, 8, 128), F32),
            pltpu.VMEM((n_tm, 2, cap), F32),
            pltpu.VMEM((n_tm, 2, cap), F32),
            pltpu.VMEM((n_tm, 1, cap), F32),
            pltpu.VMEM((n_tm, 1, cap), F32),
            pltpu.VMEM((n_src, 8, 128), F32),
            pltpu.VMEM((n_src, 8, 128), F32),
            pltpu.VMEM((n_src, 1, 128), F32),
            pltpu.VMEM((n_tm, 1, 128), F32),
            pltpu.VMEM((n_src, 1, 128), F32),
            pltpu.VMEM((n_tm, 1, 128), F32),
            pltpu.VMEM((n_tm, 128, cap), BF16),
            pltpu.VMEM((n_tm, 256, cap), BF16),
            pltpu.VMEM((n_tm, 9, 16, cap), BF16),
            pltpu.SemaphoreType.DMA((13,)),
        ]
        + [pltpu.SemaphoreType.DMA((5,))] + [pltpu.SemaphoreType.DMA((2,))] * 7,
        compiler_params=pltpu.CompilerParams(collective_id=0, has_side_effects=True),
    )(
        left_vector,
        source_coeffs,
        knot_coeffs,
        source_index,
        band_start,
        source_vector,
        knot_vector,
        bucket_fill.reshape(buckets),
        recurrence,
        source_search,
        knot_search,
        source_solution,
        knot_solution,
    )
    held = [pltpu.with_memory_space_constraint(v, pltpu.VMEM) for v in held]
    outs = pl.pallas_call(
        finish,
        out_shape=(
            jax.ShapeDtypeStruct((buckets, cap), F32),
            jax.ShapeDtypeStruct((5, source_dev), F32),
            jax.ShapeDtypeStruct((3, 1, knot_dev), F32),
            jax.ShapeDtypeStruct((5, source_dev), F32),
            jax.ShapeDtypeStruct((3, 1, knot_dev), F32),
            jax.ShapeDtypeStruct((5, source_dev), F32),
            jax.ShapeDtypeStruct((3, 1, knot_dev), F32),
            jax.ShapeDtypeStruct((1, 4), F32),
        ),
        in_specs=[vmem] * 8,
        out_specs=[vmem] * 8,
    )(*held)
    return (*outs[:7], outs[7].reshape(4))


def solution(mesh):
    in_specs = (
        P(None, ("src", "tm")),
        P(None, None, ("src", "tm")),
        P(None, None, ("src", "tm")),
        P(None, ("src", "tm")),
        P(None, ("src", "tm")),
        P(None, ("src", "tm")),
        P(None, ("src", "tm")),
        P(None, "tm", "src"),
        P(None, ("src", "tm")),
        P(None, "tm", "src"),
        P(None, ("src", "tm")),
        P(None, "tm", "src"),
        P(),
    )
    out_specs = (
        P(None, ("src", "tm")),
        P(None, ("src", "tm")),
        P(None, "tm", "src"),
        P(None, ("src", "tm")),
        P(None, "tm", "src"),
        P(None, ("src", "tm")),
        P(None, "tm", "src"),
        P(),
    )
    return jax.shard_map(shards, mesh=mesh, in_specs=in_specs, out_specs=out_specs, check_vma=False)
```

```python
import functools

import jax
import jax.numpy as jnp
from jax import lax
from jax.experimental import pallas as pl
from jax.experimental.pallas import tpu as pltpu
from jax.sharding import PartitionSpec as P

N_X = 4
FAR = 5
EPSILON = 1e-06
F32 = jnp.float32
BF16 = jnp.bfloat16
NT = (((1,), (1,)), ((), ()))
NN = (((1,), (0,)), ((), ()))


def split3(x):
    hi = x.astype(BF16)
    rest = x - hi.astype(F32)
    mid = rest.astype(BF16)
    low = (rest - mid.astype(F32)).astype(BF16)
    return hi, mid, low


def split3_f32(x):
    return [part.astype(F32) for part in split3(x)]


def iterate(
    n_src,
    n_tm,
    total_obs,
    unknowns,
    left_hbm,
    sc_hbm,
    kc_hbm,
    si_hbm,
    bs_hbm,
    sv_hbm,
    kv_hbm,
    fill_hbm,
    rec_hbm,
    ss_hbm,
    ks_hbm,
    sx_hbm,
    kx_hbm,
    raw_out,
    sraw_out,
    kraw_out,
    scal_out,
    ss_out,
    ks_out,
    sx_out,
    kx_out,
    left_ref,
    sc_ref,
    kc_ref,
    si_ref,
    bs_ref,
    sv_ref,
    kv_ref,
    fill_ref,
    rec_ref,
    ag,
    pbuf,
    prcv,
    rbuf,
    rrcv,
    rs_send,
    rs_recv,
    legs,
    joined,
    ar1a,
    ar1b,
    ar2a,
    ar2b,
    ohs,
    ohk,
    cl,
    load_sem,
    ag_sem,
    p_sem,
    r_sem,
    rs_sem,
    ar1a_sem,
    ar1b_sem,
    ar2a_sem,
    ar2b_sem,
):
    s = lax.axis_index("src")
    m = lax.axis_index("tm")
    ratio = unknowns / total_obs
    cap = left_ref.shape[1]
    n_z = n_src // N_X
    z = lax.div(s, N_X)
    x = lax.rem(s, N_X)
    pending = []

    src_order = [n_src // 2] + [sign * d for d in range(n_src // 2 - 1, 0, -1) for sign in (1, -1)]
    tm_order = list(range(1, n_tm))

    def send_all(axis, order, me, n, src, dst, sems):
        for d in order:
            o = lax.rem(me + d + n, n)
            pltpu.make_async_remote_copy(
                src_ref=src(o),
                dst_ref=dst,
                send_sem=sems.at[0],
                recv_sem=sems.at[1],
                device_id={axis: o},
                device_id_type=pl.DeviceIdType.MESH,
            ).start()

    def arrived(axis, whole, sems, which):
        copy = pltpu.make_async_remote_copy(
            src_ref=whole,
            dst_ref=whole,
            send_sem=sems.at[0],
            recv_sem=sems.at[1],
            device_id={axis: 0},
            device_id_type=pl.DeviceIdType.MESH,
        )
        return copy.wait_recv() if which else copy.wait_send()

    def src_send(src, dst, whole, sems):
        send_all("src", src_order, s, n_src, src, dst, sems)
        pending.append(lambda: arrived("src", whole, sems, 0))

    def tm_send(src, dst, whole, sems):
        send_all("tm", tm_order, m, n_tm, src, dst, sems)
        pending.append(lambda: arrived("tm", whole, sems, 0))

    src_rest = pl.ds(0, n_src - 1)
    tm_rest = pl.ds(0, n_tm - 1)
    six = pl.ds(0, 6)

    def at(dz, dx):
        return lax.rem(z + dz + n_z, n_z) * N_X + lax.rem(x + dx, N_X)

    near = [(dz, dx) for dz in (4, -4, 3, -3, 2, -2, 1, -1, 0) for dx in (2, 1, 3, 0) if dz or dx]

    loads = [
        pltpu.make_async_copy(src, dst, load_sem.at[n])
        for n, (src, dst) in enumerate(
            (
                (kv_hbm, kv_ref),
                (rec_hbm, rec_ref),
                (fill_hbm, fill_ref),
                (sv_hbm, sv_ref),
                (si_hbm, si_ref),
                (sc_hbm, sc_ref),
                (left_hbm, left_ref),
                (bs_hbm, bs_ref),
                (kc_hbm, kc_ref),
                (ss_hbm, ss_out),
                (ks_hbm, ks_out),
                (sx_hbm, sx_out),
                (kx_hbm, kx_out),
            )
        )
    ]
    for load in loads:
        load.start()

    far = [d for d in range(8, FAR - 1, -1)] + [-d for d in range(7, FAR - 1, -1)]

    barrier = pltpu.get_barrier_semaphore()
    for dz, dx in near:
        pl.semaphore_signal(barrier, inc=1, device_id={"src": at(dz, dx)}, device_id_type=pl.DeviceIdType.MESH)
    for d in tm_order:
        pl.semaphore_signal(
            barrier, inc=1, device_id={"tm": lax.rem(m + d, n_tm)}, device_id_type=pl.DeviceIdType.MESH
        )

    loads[0].wait()
    for a in range(3):
        for sub in range(2):
            ag[s, a * 2 + sub : a * 2 + sub + 1, :] = kv_ref[a, :, sub * 128 : (sub + 1) * 128]

    pl.semaphore_wait(barrier, len(near) + n_tm - 1)

    def hand_on(block, target, which):
        pltpu.make_async_remote_copy(
            src_ref=block,
            dst_ref=block,
            send_sem=ag_sem.at[0],
            recv_sem=ag_sem.at[which],
            device_id={"src": target},
            device_id_type=pl.DeviceIdType.MESH,
        ).start()

    def taken(blocks, which):
        whole = ag.at[pl.ds(0, blocks), six]
        copy = pltpu.make_async_remote_copy(
            src_ref=whole,
            dst_ref=whole,
            send_sem=ag_sem.at[0],
            recv_sem=ag_sem.at[which],
            device_id={"src": s},
            device_id_type=pl.DeviceIdType.MESH,
        )
        return copy.wait_recv() if which else copy.wait_send()

    for dz, dx in near:
        hand_on(ag.at[s, six], at(dz, dx), 1 if dz == 4 else 2 if dz == -4 else 3)
    pending.append(lambda: taken(n_src - 1, 0))
    for load in loads[1:7]:
        load.wait()

    alpha = rec_ref[0]
    pad3 = jnp.zeros((3, 128), F32)
    table = jnp.concatenate(
        [jnp.concatenate([sv_ref[:, l * 128 : (l + 1) * 128], pad3], axis=0) for l in range(8)], axis=0
    )
    stable = jnp.concatenate(split3(table), axis=1)
    rows128 = lax.broadcasted_iota(jnp.int32, (128, cap), 0)
    lane = lax.broadcasted_iota(jnp.int32, (1, cap), 1)

    for t in range(n_tm):
        idx = si_ref[t : t + 1, :]
        hi = jnp.bitwise_and(idx, 127)
        lo = jnp.right_shift(idx, 7)
        oh = jnp.where(rows128 == hi, 1.0, 0.0).astype(BF16)
        ohs[t] = oh
        found = lax.dot_general(
            stable, jnp.concatenate([oh, oh, oh], axis=0), NN, preferred_element_type=F32
        )
        picked = jnp.zeros((8, cap), F32)
        for l in range(8):
            picked = picked + jnp.where(lo == l, found[l * 8 : (l + 1) * 8], 0.0)
        coef = sc_ref[:, t, :]
        image = jnp.sum(coef * picked[0:5], axis=0, keepdims=True)
        pbuf[t, 0:1, :] = image - alpha * left_ref[t : t + 1, :]
        pbuf[t, 1:2, :] = jnp.where(lane < fill_ref[t], 1.0, 0.0)

    tm_send(lambda o: pbuf.at[o], prcv.at[m], pbuf.at[tm_rest], p_sem)
    prcv[m] = pbuf[m]
    for which, sign, reach in ((1, 1, 4), (2, -1, 3)):
        taken(N_X, which)
        plane = ag.at[pl.ds(lax.rem(z - sign * 4 + n_z, n_z) * N_X, N_X), six]
        for k in range(reach, 0, -1):
            hand_on(plane, at(sign * k, 0), 4)

    for load in loads[7:]:
        load.wait()

    for dz in far:
        rs_recv[pl.ds(at(dz, 0) - x, N_X)] = jnp.zeros((N_X, 8, 128), F32)

    rows256 = lax.broadcasted_iota(jnp.int32, (256, cap), 0)
    for i in range(n_tm):
        band = bs_ref[i : i + 1, :]
        hi = (
            jnp.bitwise_and(jnp.right_shift(band, 4), 1) * 128
            + jnp.bitwise_and(jnp.right_shift(band, 5), 1) * 64
            + jnp.right_shift(band, 6)
        )
        ohk[i] = jnp.where(rows256 == hi, 1.0, 0.0).astype(BF16)

    arrived("tm", prcv.at[tm_rest], p_sem, 1)
    taken(len(near) - 2 * N_X, 3)
    taken(7 * N_X, 4)

    table = []
    for a in range(3):
        whole = jnp.concatenate([ag[:, a * 2 + half, :] for half in range(2)], axis=0)
        turned = jnp.transpose(whole)
        table.append(jnp.concatenate([turned[0:64], turned[64:128]], axis=1))
    ktable = jnp.concatenate(split3(jnp.concatenate(table, axis=0)), axis=0)

    band_rows = jnp.right_shift(lax.broadcasted_iota(jnp.int32, (64, cap), 0), 2)
    total = jnp.zeros((1, cap), F32)
    for i in range(n_tm):
        three = lax.dot_general(ktable, ohk[i], NN, preferred_element_type=F32)
        found = three[0:192] + three[192:384] + three[384:576]
        lo = jnp.bitwise_and(bs_ref[i : i + 1, :], 15)
        coefs = []
        mixed = None
        for a in range(3):
            four = kc_ref[a * 4 : a * 4 + 4, i, :]
            eight = jnp.concatenate([four, four], axis=0)
            coefs.append(eight)
            term = found[a * 64 : (a + 1) * 64].reshape(8, 8, cap) * eight[None]
            mixed = term if mixed is None else mixed + term
        image = jnp.sum(jnp.where(band_rows == lo, mixed.reshape(64, cap), 0.0), axis=0, keepdims=True)
        raw = prcv[i, 1:2, :] * (prcv[i, 0:1, :] + image)
        rbuf[i] = raw
        total = total + raw * raw
        for a in range(3):
            for q, part in enumerate(split3_f32(coefs[a] * raw)):
                cl[i, q * 3 + a] = jnp.concatenate([part, part], axis=0).astype(BF16)
    ar1a[s] = total[:, 0:128] + total[:, 128:256]
    src_send(lambda o: ar1a.at[s], ar1a.at[s], ar1a.at[src_rest], ar1a_sem)
    tm_send(lambda o: rbuf.at[o], rrcv.at[m], rbuf.at[tm_rest], r_sem)
    rrcv[m] = rbuf[m]

    acc = jnp.zeros((192, 256), F32)
    for i in range(n_tm):
        lo = jnp.bitwise_and(bs_ref[i : i + 1, :], 15)
        hit = jnp.where(band_rows == lo, 1.0, 0.0).astype(BF16)
        terms = jnp.concatenate(
            [hit * jnp.concatenate([cl[i, row]] * 4, axis=0) for row in range(9)], axis=0
        )
        three = lax.dot_general(terms, ohk[i], NT, preferred_element_type=F32)
        acc = acc + (three[0:192] + three[192:384] + three[384:576])
    for a in range(3):
        own = acc[a * 64 : (a + 1) * 64]
        turned = jnp.transpose(jnp.concatenate([own[:, 0:128], own[:, 128:256]], axis=0))
        for half in range(2):
            rs_send[:, a * 2 + half, :] = turned[half * 64 : (half + 1) * 64]

    def add_up(block, target, slot, which):
        pltpu.make_async_remote_copy(
            src_ref=block,
            dst_ref=slot,
            send_sem=rs_sem.at[0],
            recv_sem=rs_sem.at[which],
            device_id={"src": target},
            device_id_type=pl.DeviceIdType.MESH,
        ).start()

    for n, dz in enumerate(far):
        short = 4 if dz > 0 else -4
        plane = pl.ds(at(dz, 0) - x, N_X)
        add_up(rs_send.at[plane, six], at(dz - short, 0), legs.at[n, :, six], 2)
    for dz in [sign * d for d in range(FAR - 1, 0, -1) for sign in (1, -1) if d != 4] + [0]:
        for dx in (2, 1, 3, 0):
            if dz or dx:
                add_up(rs_send.at[at(dz, dx), six], at(dz, dx), rs_recv.at[s, six], 1)
    pending.append(lambda: arrived("src", rs_send.at[src_rest, six], rs_sem, 0))
    whole = legs.at[:, :, six]
    pltpu.make_async_remote_copy(
        src_ref=whole,
        dst_ref=whole,
        send_sem=rs_sem.at[0],
        recv_sem=rs_sem.at[2],
        device_id={"src": s},
        device_id_type=pl.DeviceIdType.MESH,
    ).wait_recv()
    for n, sign in enumerate((1, -1)):
        added = rs_send[pl.ds(at(4 * sign, 0) - x, N_X)]
        for leg, dz in enumerate(far):
            if dz * sign > 0:
                added = added + legs[leg]
        joined[n] = added
    for dx in (2, 1, 3, 0):
        for n, sign in enumerate((1, -1)):
            target = at(4 * sign, dx)
            add_up(joined.at[n, lax.rem(x + dx, N_X), six], target, rs_recv.at[s, six], 1)
    rs_recv[s] = rs_send[s]
    arrived("tm", rrcv.at[tm_rest], r_sem, 1)

    grad = jnp.zeros((64, 128), F32)
    for t in range(n_tm):
        raw = rrcv[t]
        raw_out[t : t + 1, :] = raw
        lo = jnp.right_shift(si_ref[t : t + 1, :], 7)
        coef = jnp.concatenate([sc_ref[:, t, :], jnp.zeros((3, cap), F32)], axis=0)
        spread = []
        for part in split3_f32(coef * raw):
            spread.append(
                jnp.concatenate([jnp.where(lo == l, part, 0.0) for l in range(8)], axis=0).astype(BF16)
            )
        oh = ohs[t]
        grad = grad + lax.dot_general(
            jnp.concatenate(spread, axis=1),
            jnp.concatenate([oh, oh, oh], axis=1),
            NT,
            preferred_element_type=F32,
        )

    arrived("src", ar1a.at[src_rest], ar1a_sem, 1)
    ar1b[m] = jnp.sum(ar1a[...], axis=0)
    tm_send(lambda o: ar1b.at[m], ar1b.at[m], ar1b.at[tm_rest], ar1b_sem)
    arrived("tm", ar1b.at[tm_rest], ar1b_sem, 1)
    beta = jnp.sqrt(jnp.sum(jnp.sum(ar1b[...], axis=0), axis=1, keepdims=True) / total_obs + EPSILON)
    scale = ratio / beta
    squares = jnp.zeros((1, 128), F32)
    for l in range(8):
        own = scale * grad[l * 8 : l * 8 + 5] - beta * sv_ref[:, l * 128 : (l + 1) * 128]
        sraw_out[:, l * 128 : (l + 1) * 128] = own
        squares = squares + jnp.sum(own * own, axis=0, keepdims=True)

    arrived("src", rs_recv.at[pl.ds(0, n_src - 1 - N_X * len(far)), six], rs_sem, 1)
    gathered = jnp.sum(rs_recv[...], axis=0)
    for a in range(3):
        for sub in range(2):
            row = a * 2 + sub
            own = scale * gathered[row : row + 1] - beta * kv_ref[a, :, sub * 128 : (sub + 1) * 128]
            kraw_out[a, :, sub * 128 : (sub + 1) * 128] = own
            squares = squares + own * own

    ar2b[m] = squares
    tm_send(lambda o: ar2b.at[m], ar2b.at[m], ar2b.at[tm_rest], ar2b_sem)
    arrived("tm", ar2b.at[tm_rest], ar2b_sem, 1)
    ar2a[s] = jnp.sum(ar2b[...], axis=0)
    src_send(lambda o: ar2a.at[s], ar2a.at[s], ar2a.at[src_rest], ar2a_sem)
    arrived("src", ar2a.at[src_rest], ar2a_sem, 1)
    alpha_next = jnp.sqrt(
        jnp.sum(jnp.sum(ar2a[...], axis=0), axis=1, keepdims=True) / unknowns + EPSILON
    )
    pivot = rec_ref[1]
    remainder = rec_ref[2]
    radius = jnp.sqrt(pivot * pivot + beta * beta)
    cosine = pivot / radius
    sine = beta / radius
    wide = (1, 128)
    lane = lax.broadcasted_iota(jnp.int32, wide, 1)
    scal_out[0:1, :] = jnp.broadcast_to(alpha_next, wide)
    scal_out[1:2, :] = jnp.broadcast_to(beta, wide)
    scal_out[2:3, :] = jnp.broadcast_to(cosine * remainder / radius, wide)
    scal_out[3:4, :] = jnp.broadcast_to(sine * alpha_next / radius, wide)
    scal_out[4:5, :] = jnp.where(
        lane == 0,
        alpha_next,
        jnp.where(lane == 1, beta, jnp.where(lane == 2, -cosine * alpha_next, sine * remainder)),
    )
    for wait in pending:
        wait()


def finish(
    raw_ref,
    sraw_ref,
    kraw_ref,
    scal_ref,
    ss_ref,
    ks_ref,
    sx_ref,
    kx_ref,
    left_out,
    snext_out,
    knext_out,
    ssearch_out,
    ksearch_out,
    sx_out,
    kx_out,
    rec_out,
):
    alpha_next = scal_ref[0:1, 0:1]
    beta = scal_ref[1:2, 0:1]
    gain = scal_ref[2:3, 0:1]
    share = scal_ref[3:4, 0:1]
    left_out[...] = raw_ref[...] / beta
    snext = sraw_ref[...] / alpha_next
    snext_out[...] = snext
    ssearch_out[...] = snext - share * ss_ref[...]
    sx_out[...] = sx_ref[...] + gain * ss_ref[...]
    for a in range(3):
        knext = kraw_ref[a] / alpha_next
        knext_out[a] = knext
        ksearch_out[a] = knext - share * ks_ref[a]
        kx_out[a] = kx_ref[a] + gain * ks_ref[a]
    rec_out[...] = scal_ref[4:5, 0:4]


def shards(
    left_vector,
    source_coeffs,
    knot_coeffs,
    source_index,
    band_start,
    bucket_fill,
    source_vector,
    knot_vector,
    source_search,
    knot_search,
    source_solution,
    knot_solution,
    recurrence,
):
    n_tm = lax.axis_size("tm")
    n_src = lax.axis_size("src")
    devices = n_tm * n_src
    buckets, cap = left_vector.shape
    source_dev = source_vector.shape[1]
    knot_dev = knot_vector.shape[2]
    total_obs = buckets * cap * devices
    unknowns = (5 * source_dev + 3 * knot_dev) * devices
    vmem = pl.BlockSpec(memory_space=pltpu.VMEM)
    hbm = pl.BlockSpec(memory_space=pl.ANY)
    held = pl.pallas_call(
        functools.partial(iterate, n_src, n_tm, total_obs, unknowns),
        out_shape=(
            pltpu.VMEM((buckets, cap), F32),
            pltpu.VMEM((5, source_dev), F32),
            pltpu.VMEM((3, 1, knot_dev), F32),
            pltpu.VMEM((8, 128), F32),
            pltpu.VMEM((5, source_dev), F32),
            pltpu.VMEM((3, 1, knot_dev), F32),
            pltpu.VMEM((5, source_dev), F32),
            pltpu.VMEM((3, 1, knot_dev), F32),
        ),
        in_specs=[hbm] * 13,
        out_specs=[vmem] * 8,
        scratch_shapes=[
            pltpu.VMEM(a.shape, a.dtype)
            for a in (
                left_vector,
                source_coeffs,
                knot_coeffs,
                source_index,
                band_start,
                source_vector,
                knot_vector,
            )
        ]
        + [
            pltpu.SMEM((buckets,), jnp.int32),
            pltpu.SMEM((3,), F32),
            pltpu.VMEM((n_src, 8, 128), F32),
            pltpu.VMEM((n_tm, 2, cap), F32),
            pltpu.VMEM((n_tm, 2, cap), F32),
            pltpu.VMEM((n_tm, 1, cap), F32),
            pltpu.VMEM((n_tm, 1, cap), F32),
            pltpu.VMEM((n_src, 8, 128), F32),
            pltpu.VMEM((n_src, 8, 128), F32),
            pltpu.VMEM((17 - 2 * FAR, N_X, 8, 128), F32),
            pltpu.VMEM((2, N_X, 8, 128), F32),
            pltpu.VMEM((n_src, 1, 128), F32),
            pltpu.VMEM((n_tm, 1, 128), F32),
            pltpu.VMEM((n_src, 1, 128), F32),
            pltpu.VMEM((n_tm, 1, 128), F32),
            pltpu.VMEM((n_tm, 128, cap), BF16),
            pltpu.VMEM((n_tm, 256, cap), BF16),
            pltpu.VMEM((n_tm, 9, 16, cap), BF16),
            pltpu.SemaphoreType.DMA((13,)),
        ]
        + [pltpu.SemaphoreType.DMA((5,))]
        + [pltpu.SemaphoreType.DMA((3,))] * 7,
        compiler_params=pltpu.CompilerParams(collective_id=0, has_side_effects=True),
    )(
        left_vector,
        source_coeffs,
        knot_coeffs,
        source_index,
        band_start,
        source_vector,
        knot_vector,
        bucket_fill.reshape(buckets),
        recurrence,
        source_search,
        knot_search,
        source_solution,
        knot_solution,
    )
    held = [pltpu.with_memory_space_constraint(v, pltpu.VMEM) for v in held]
    outs = pl.pallas_call(
        finish,
        out_shape=(
            jax.ShapeDtypeStruct((buckets, cap), F32),
            jax.ShapeDtypeStruct((5, source_dev), F32),
            jax.ShapeDtypeStruct((3, 1, knot_dev), F32),
            jax.ShapeDtypeStruct((5, source_dev), F32),
            jax.ShapeDtypeStruct((3, 1, knot_dev), F32),
            jax.ShapeDtypeStruct((5, source_dev), F32),
            jax.ShapeDtypeStruct((3, 1, knot_dev), F32),
            jax.ShapeDtypeStruct((1, 4), F32),
        ),
        in_specs=[vmem] * 8,
        out_specs=[vmem] * 8,
    )(*held)
    return (*outs[:7], outs[7].reshape(4))


def solution(mesh):
    in_specs = (
        P(None, ("src", "tm")),
        P(None, None, ("src", "tm")),
        P(None, None, ("src", "tm")),
        P(None, ("src", "tm")),
        P(None, ("src", "tm")),
        P(None, ("src", "tm")),
        P(None, ("src", "tm")),
        P(None, "tm", "src"),
        P(None, ("src", "tm")),
        P(None, "tm", "src"),
        P(None, ("src", "tm")),
        P(None, "tm", "src"),
        P(),
    )
    out_specs = (
        P(None, ("src", "tm")),
        P(None, ("src", "tm")),
        P(None, "tm", "src"),
        P(None, ("src", "tm")),
        P(None, "tm", "src"),
        P(None, ("src", "tm")),
        P(None, "tm", "src"),
        P(),
    )
    return jax.shard_map(shards, mesh=mesh, in_specs=in_specs, out_specs=out_specs, check_vma=False)
```

```python
import functools

import jax
import jax.numpy as jnp
from jax import lax
from jax.experimental import pallas as pl
from jax.experimental.pallas import tpu as pltpu
from jax.sharding import PartitionSpec as P

N_X = 4
FAR = 5
EPSILON = 1e-06
F32 = jnp.float32
BF16 = jnp.bfloat16
NT = (((1,), (1,)), ((), ()))
NN = (((1,), (0,)), ((), ()))


def split3(x):
    hi = x.astype(BF16)
    rest = x - hi.astype(F32)
    mid = rest.astype(BF16)
    low = (rest - mid.astype(F32)).astype(BF16)
    return hi, mid, low


def split3_f32(x):
    return [part.astype(F32) for part in split3(x)]


def iterate(
    n_src,
    n_tm,
    total_obs,
    unknowns,
    left_hbm,
    sc_hbm,
    kc_hbm,
    si_hbm,
    bs_hbm,
    sv_hbm,
    kv_hbm,
    fill_hbm,
    rec_hbm,
    ss_hbm,
    ks_hbm,
    sx_hbm,
    kx_hbm,
    raw_out,
    sraw_out,
    kraw_out,
    scal_out,
    ss_out,
    ks_out,
    sx_out,
    kx_out,
    left_ref,
    sc_ref,
    kc_ref,
    si_ref,
    bs_ref,
    sv_ref,
    kv_ref,
    fill_ref,
    rec_ref,
    ag,
    pbuf,
    prcv,
    rbuf,
    rrcv,
    rs_send,
    rs_recv,
    legs,
    joined,
    ar1a,
    ar1b,
    ar2a,
    ar2b,
    ohs,
    ohk,
    cl,
    load_sem,
    ag_sem,
    p_sem,
    r_sem,
    rs_sem,
    ar1a_sem,
    ar1b_sem,
    ar2a_sem,
    ar2b_sem,
):
    s = lax.axis_index("src")
    m = lax.axis_index("tm")
    ratio = unknowns / total_obs
    cap = left_ref.shape[1]
    n_z = n_src // N_X
    z = lax.div(s, N_X)
    x = lax.rem(s, N_X)
    pending = []

    src_order = [n_src // 2] + [sign * d for d in range(n_src // 2 - 1, 0, -1) for sign in (1, -1)]
    tm_order = list(range(1, n_tm))

    def send_all(axis, order, me, n, src, dst, sems):
        for d in order:
            o = lax.rem(me + d + n, n)
            pltpu.make_async_remote_copy(
                src_ref=src(o),
                dst_ref=dst,
                send_sem=sems.at[0],
                recv_sem=sems.at[1],
                device_id={axis: o},
                device_id_type=pl.DeviceIdType.MESH,
            ).start()

    def arrived(axis, whole, sems, which):
        copy = pltpu.make_async_remote_copy(
            src_ref=whole,
            dst_ref=whole,
            send_sem=sems.at[0],
            recv_sem=sems.at[1],
            device_id={axis: 0},
            device_id_type=pl.DeviceIdType.MESH,
        )
        return copy.wait_recv() if which else copy.wait_send()

    def src_send(src, dst, whole, sems):
        send_all("src", src_order, s, n_src, src, dst, sems)
        pending.append(lambda: arrived("src", whole, sems, 0))

    def tm_send(src, dst, whole, sems):
        send_all("tm", tm_order, m, n_tm, src, dst, sems)
        pending.append(lambda: arrived("tm", whole, sems, 0))

    plane_size = N_X * n_tm
    spot = x * n_tm + m
    plane_peers = [(dx, dm) for dx in (2, 1, 3, 0) for dm in (4, 3, 5, 2, 6, 7, 1, 0) if dx or dm]
    line_peers = [n_z // 2] + [sign * d for d in range(n_z // 2 - 1, 0, -1) for sign in (1, -1)]

    def tell(row, target, sems):
        pltpu.make_async_remote_copy(
            src_ref=row,
            dst_ref=row,
            send_sem=sems.at[0],
            recv_sem=sems.at[1],
            device_id=target,
            device_id_type=pl.DeviceIdType.MESH,
        ).start()

    def plane_send(buf, sems):
        for dx, dm in plane_peers:
            tell(buf.at[spot], {"src": z * N_X + lax.rem(x + dx, N_X), "tm": lax.rem(m + dm, n_tm)}, sems)
        pending.append(lambda: arrived("src", buf.at[pl.ds(0, plane_size - 1)], sems, 0))

    def line_send(buf, sems):
        for dz in line_peers:
            tell(buf.at[z], {"src": lax.rem(z + dz + n_z, n_z) * N_X + x}, sems)
        pending.append(lambda: arrived("src", buf.at[pl.ds(0, n_z - 1)], sems, 0))

    src_rest = pl.ds(0, n_src - 1)
    tm_rest = pl.ds(0, n_tm - 1)
    plane_rest = pl.ds(0, plane_size - 1)
    line_rest = pl.ds(0, n_z - 1)
    six = pl.ds(0, 6)

    def at(dz, dx):
        return lax.rem(z + dz + n_z, n_z) * N_X + lax.rem(x + dx, N_X)

    near = [(dz, dx) for dz in (4, -4, 3, -3, 2, -2, 1, -1, 0) for dx in (2, 1, 3, 0) if dz or dx]

    loads = [
        pltpu.make_async_copy(src, dst, load_sem.at[n])
        for n, (src, dst) in enumerate(
            (
                (kv_hbm, kv_ref),
                (rec_hbm, rec_ref),
                (fill_hbm, fill_ref),
                (sv_hbm, sv_ref),
                (si_hbm, si_ref),
                (sc_hbm, sc_ref),
                (left_hbm, left_ref),
                (bs_hbm, bs_ref),
                (kc_hbm, kc_ref),
                (ss_hbm, ss_out),
                (ks_hbm, ks_out),
                (sx_hbm, sx_out),
                (kx_hbm, kx_out),
            )
        )
    ]
    for load in loads:
        load.start()

    far = [d for d in range(8, FAR - 1, -1)] + [-d for d in range(7, FAR - 1, -1)]

    barrier = pltpu.get_barrier_semaphore()
    for dz, dx in near:
        pl.semaphore_signal(barrier, inc=1, device_id={"src": at(dz, dx)}, device_id_type=pl.DeviceIdType.MESH)
    for d in tm_order:
        pl.semaphore_signal(
            barrier, inc=1, device_id={"tm": lax.rem(m + d, n_tm)}, device_id_type=pl.DeviceIdType.MESH
        )

    loads[0].wait()
    for a in range(3):
        for sub in range(2):
            ag[s, a * 2 + sub : a * 2 + sub + 1, :] = kv_ref[a, :, sub * 128 : (sub + 1) * 128]

    pl.semaphore_wait(barrier, len(near) + n_tm - 1)

    def hand_on(block, target, which):
        pltpu.make_async_remote_copy(
            src_ref=block,
            dst_ref=block,
            send_sem=ag_sem.at[0],
            recv_sem=ag_sem.at[which],
            device_id={"src": target},
            device_id_type=pl.DeviceIdType.MESH,
        ).start()

    def taken(blocks, which):
        whole = ag.at[pl.ds(0, blocks), six]
        copy = pltpu.make_async_remote_copy(
            src_ref=whole,
            dst_ref=whole,
            send_sem=ag_sem.at[0],
            recv_sem=ag_sem.at[which],
            device_id={"src": s},
            device_id_type=pl.DeviceIdType.MESH,
        )
        return copy.wait_recv() if which else copy.wait_send()

    for dz, dx in near:
        hand_on(ag.at[s, six], at(dz, dx), 1 if dz == 4 else 2 if dz == -4 else 3)
    pending.append(lambda: taken(n_src - 1, 0))
    for load in loads[1:7]:
        load.wait()

    alpha = rec_ref[0]
    pad3 = jnp.zeros((3, 128), F32)
    table = jnp.concatenate(
        [jnp.concatenate([sv_ref[:, l * 128 : (l + 1) * 128], pad3], axis=0) for l in range(8)], axis=0
    )
    stable = jnp.concatenate(split3(table), axis=1)
    rows128 = lax.broadcasted_iota(jnp.int32, (128, cap), 0)
    lane = lax.broadcasted_iota(jnp.int32, (1, cap), 1)

    for t in range(n_tm):
        idx = si_ref[t : t + 1, :]
        hi = jnp.bitwise_and(idx, 127)
        lo = jnp.right_shift(idx, 7)
        oh = jnp.where(rows128 == hi, 1.0, 0.0).astype(BF16)
        ohs[t] = oh
        found = lax.dot_general(
            stable, jnp.concatenate([oh, oh, oh], axis=0), NN, preferred_element_type=F32
        )
        picked = jnp.zeros((8, cap), F32)
        for l in range(8):
            picked = picked + jnp.where(lo == l, found[l * 8 : (l + 1) * 8], 0.0)
        coef = sc_ref[:, t, :]
        image = jnp.sum(coef * picked[0:5], axis=0, keepdims=True)
        pbuf[t, 0:1, :] = image - alpha * left_ref[t : t + 1, :]
        pbuf[t, 1:2, :] = jnp.where(lane < fill_ref[t], 1.0, 0.0)

    tm_send(lambda o: pbuf.at[o], prcv.at[m], pbuf.at[tm_rest], p_sem)
    prcv[m] = pbuf[m]
    for which, sign, reach in ((1, 1, 4), (2, -1, 3)):
        taken(N_X, which)
        plane = ag.at[pl.ds(lax.rem(z - sign * 4 + n_z, n_z) * N_X, N_X), six]
        for k in range(reach, 0, -1):
            hand_on(plane, at(sign * k, 0), 4)

    for load in loads[7:]:
        load.wait()

    for dz in far:
        rs_recv[pl.ds(at(dz, 0) - x, N_X)] = jnp.zeros((N_X, 8, 128), F32)

    rows256 = lax.broadcasted_iota(jnp.int32, (256, cap), 0)
    for i in range(n_tm):
        band = bs_ref[i : i + 1, :]
        hi = (
            jnp.bitwise_and(jnp.right_shift(band, 4), 1) * 128
            + jnp.bitwise_and(jnp.right_shift(band, 5), 1) * 64
            + jnp.right_shift(band, 6)
        )
        ohk[i] = jnp.where(rows256 == hi, 1.0, 0.0).astype(BF16)

    arrived("tm", prcv.at[tm_rest], p_sem, 1)
    taken(len(near) - 2 * N_X, 3)
    taken(7 * N_X, 4)

    table = []
    for a in range(3):
        whole = jnp.concatenate([ag[:, a * 2 + half, :] for half in range(2)], axis=0)
        turned = jnp.transpose(whole)
        table.append(jnp.concatenate([turned[0:64], turned[64:128]], axis=1))
    ktable = jnp.concatenate(split3(jnp.concatenate(table, axis=0)), axis=0)

    band_rows = jnp.right_shift(lax.broadcasted_iota(jnp.int32, (64, cap), 0), 2)
    total = jnp.zeros((1, cap), F32)
    for i in range(n_tm):
        three = lax.dot_general(ktable, ohk[i], NN, preferred_element_type=F32)
        found = three[0:192] + three[192:384] + three[384:576]
        lo = jnp.bitwise_and(bs_ref[i : i + 1, :], 15)
        coefs = []
        mixed = None
        for a in range(3):
            four = kc_ref[a * 4 : a * 4 + 4, i, :]
            eight = jnp.concatenate([four, four], axis=0)
            coefs.append(eight)
            term = found[a * 64 : (a + 1) * 64].reshape(8, 8, cap) * eight[None]
            mixed = term if mixed is None else mixed + term
        image = jnp.sum(jnp.where(band_rows == lo, mixed.reshape(64, cap), 0.0), axis=0, keepdims=True)
        raw = prcv[i, 1:2, :] * (prcv[i, 0:1, :] + image)
        rbuf[i] = raw
        total = total + raw * raw
        for a in range(3):
            for q, part in enumerate(split3_f32(coefs[a] * raw)):
                cl[i, q * 3 + a] = jnp.concatenate([part, part], axis=0).astype(BF16)
    ar1a[s] = total[:, 0:128] + total[:, 128:256]
    src_send(lambda o: ar1a.at[s], ar1a.at[s], ar1a.at[src_rest], ar1a_sem)
    tm_send(lambda o: rbuf.at[o], rrcv.at[m], rbuf.at[tm_rest], r_sem)
    rrcv[m] = rbuf[m]

    acc = jnp.zeros((192, 256), F32)
    for i in range(n_tm):
        lo = jnp.bitwise_and(bs_ref[i : i + 1, :], 15)
        hit = jnp.where(band_rows == lo, 1.0, 0.0).astype(BF16)
        terms = jnp.concatenate(
            [hit * jnp.concatenate([cl[i, row]] * 4, axis=0) for row in range(9)], axis=0
        )
        three = lax.dot_general(terms, ohk[i], NT, preferred_element_type=F32)
        acc = acc + (three[0:192] + three[192:384] + three[384:576])
    for a in range(3):
        own = acc[a * 64 : (a + 1) * 64]
        turned = jnp.transpose(jnp.concatenate([own[:, 0:128], own[:, 128:256]], axis=0))
        for half in range(2):
            rs_send[:, a * 2 + half, :] = turned[half * 64 : (half + 1) * 64]

    def add_up(block, target, slot, which):
        pltpu.make_async_remote_copy(
            src_ref=block,
            dst_ref=slot,
            send_sem=rs_sem.at[0],
            recv_sem=rs_sem.at[which],
            device_id={"src": target},
            device_id_type=pl.DeviceIdType.MESH,
        ).start()

    for n, dz in enumerate(far):
        short = 4 if dz > 0 else -4
        plane = pl.ds(at(dz, 0) - x, N_X)
        add_up(rs_send.at[plane, six], at(dz - short, 0), legs.at[n, :, six], 2)
    for dz in [sign * d for d in range(FAR - 1, 0, -1) for sign in (1, -1) if d != 4] + [0]:
        for dx in (2, 1, 3, 0):
            if dz or dx:
                add_up(rs_send.at[at(dz, dx), six], at(dz, dx), rs_recv.at[s, six], 1)
    pending.append(lambda: arrived("src", rs_send.at[src_rest, six], rs_sem, 0))
    whole = legs.at[:, :, six]
    pltpu.make_async_remote_copy(
        src_ref=whole,
        dst_ref=whole,
        send_sem=rs_sem.at[0],
        recv_sem=rs_sem.at[2],
        device_id={"src": s},
        device_id_type=pl.DeviceIdType.MESH,
    ).wait_recv()
    for n, sign in enumerate((1, -1)):
        added = rs_send[pl.ds(at(4 * sign, 0) - x, N_X)]
        for leg, dz in enumerate(far):
            if dz * sign > 0:
                added = added + legs[leg]
        joined[n] = added
    for dx in (2, 1, 3, 0):
        for n, sign in enumerate((1, -1)):
            target = at(4 * sign, dx)
            add_up(joined.at[n, lax.rem(x + dx, N_X), six], target, rs_recv.at[s, six], 1)
    rs_recv[s] = rs_send[s]
    arrived("tm", rrcv.at[tm_rest], r_sem, 1)

    grad = jnp.zeros((64, 128), F32)
    for t in range(n_tm):
        raw = rrcv[t]
        raw_out[t : t + 1, :] = raw
        lo = jnp.right_shift(si_ref[t : t + 1, :], 7)
        coef = jnp.concatenate([sc_ref[:, t, :], jnp.zeros((3, cap), F32)], axis=0)
        spread = []
        for part in split3_f32(coef * raw):
            spread.append(
                jnp.concatenate([jnp.where(lo == l, part, 0.0) for l in range(8)], axis=0).astype(BF16)
            )
        oh = ohs[t]
        grad = grad + lax.dot_general(
            jnp.concatenate(spread, axis=1),
            jnp.concatenate([oh, oh, oh], axis=1),
            NT,
            preferred_element_type=F32,
        )

    arrived("src", ar1a.at[src_rest], ar1a_sem, 1)
    ar1b[m] = jnp.sum(ar1a[...], axis=0)
    tm_send(lambda o: ar1b.at[m], ar1b.at[m], ar1b.at[tm_rest], ar1b_sem)
    arrived("tm", ar1b.at[tm_rest], ar1b_sem, 1)
    beta = jnp.sqrt(jnp.sum(jnp.sum(ar1b[...], axis=0), axis=1, keepdims=True) / total_obs + EPSILON)
    scale = ratio / beta
    squares = jnp.zeros((1, 128), F32)
    for l in range(8):
        own = scale * grad[l * 8 : l * 8 + 5] - beta * sv_ref[:, l * 128 : (l + 1) * 128]
        sraw_out[:, l * 128 : (l + 1) * 128] = own
        squares = squares + jnp.sum(own * own, axis=0, keepdims=True)

    arrived("src", rs_recv.at[pl.ds(0, n_src - 1 - N_X * len(far)), six], rs_sem, 1)
    gathered = jnp.sum(rs_recv[...], axis=0)
    for a in range(3):
        for sub in range(2):
            row = a * 2 + sub
            own = scale * gathered[row : row + 1] - beta * kv_ref[a, :, sub * 128 : (sub + 1) * 128]
            kraw_out[a, :, sub * 128 : (sub + 1) * 128] = own
            squares = squares + own * own

    ar2a[spot] = squares
    plane_send(ar2a, ar2a_sem)
    arrived("src", ar2a.at[plane_rest], ar2a_sem, 1)
    ar2b[z] = jnp.sum(ar2a[...], axis=0)
    line_send(ar2b, ar2b_sem)
    arrived("src", ar2b.at[line_rest], ar2b_sem, 1)
    alpha_next = jnp.sqrt(
        jnp.sum(jnp.sum(ar2b[...], axis=0), axis=1, keepdims=True) / unknowns + EPSILON
    )
    pivot = rec_ref[1]
    remainder = rec_ref[2]
    radius = jnp.sqrt(pivot * pivot + beta * beta)
    cosine = pivot / radius
    sine = beta / radius
    wide = (1, 128)
    lane = lax.broadcasted_iota(jnp.int32, wide, 1)
    scal_out[0:1, :] = jnp.broadcast_to(alpha_next, wide)
    scal_out[1:2, :] = jnp.broadcast_to(beta, wide)
    scal_out[2:3, :] = jnp.broadcast_to(cosine * remainder / radius, wide)
    scal_out[3:4, :] = jnp.broadcast_to(sine * alpha_next / radius, wide)
    scal_out[4:5, :] = jnp.where(
        lane == 0,
        alpha_next,
        jnp.where(lane == 1, beta, jnp.where(lane == 2, -cosine * alpha_next, sine * remainder)),
    )
    for wait in pending:
        wait()


def finish(
    raw_ref,
    sraw_ref,
    kraw_ref,
    scal_ref,
    ss_ref,
    ks_ref,
    sx_ref,
    kx_ref,
    left_out,
    snext_out,
    knext_out,
    ssearch_out,
    ksearch_out,
    sx_out,
    kx_out,
    rec_out,
):
    alpha_next = scal_ref[0:1, 0:1]
    beta = scal_ref[1:2, 0:1]
    gain = scal_ref[2:3, 0:1]
    share = scal_ref[3:4, 0:1]
    left_out[...] = raw_ref[...] / beta
    snext = sraw_ref[...] / alpha_next
    snext_out[...] = snext
    ssearch_out[...] = snext - share * ss_ref[...]
    sx_out[...] = sx_ref[...] + gain * ss_ref[...]
    for a in range(3):
        knext = kraw_ref[a] / alpha_next
        knext_out[a] = knext
        ksearch_out[a] = knext - share * ks_ref[a]
        kx_out[a] = kx_ref[a] + gain * ks_ref[a]
    rec_out[...] = scal_ref[4:5, 0:4]


def shards(
    left_vector,
    source_coeffs,
    knot_coeffs,
    source_index,
    band_start,
    bucket_fill,
    source_vector,
    knot_vector,
    source_search,
    knot_search,
    source_solution,
    knot_solution,
    recurrence,
):
    n_tm = lax.axis_size("tm")
    n_src = lax.axis_size("src")
    devices = n_tm * n_src
    buckets, cap = left_vector.shape
    source_dev = source_vector.shape[1]
    knot_dev = knot_vector.shape[2]
    total_obs = buckets * cap * devices
    unknowns = (5 * source_dev + 3 * knot_dev) * devices
    vmem = pl.BlockSpec(memory_space=pltpu.VMEM)
    hbm = pl.BlockSpec(memory_space=pl.ANY)
    held = pl.pallas_call(
        functools.partial(iterate, n_src, n_tm, total_obs, unknowns),
        out_shape=(
            pltpu.VMEM((buckets, cap), F32),
            pltpu.VMEM((5, source_dev), F32),
            pltpu.VMEM((3, 1, knot_dev), F32),
            pltpu.VMEM((8, 128), F32),
            pltpu.VMEM((5, source_dev), F32),
            pltpu.VMEM((3, 1, knot_dev), F32),
            pltpu.VMEM((5, source_dev), F32),
            pltpu.VMEM((3, 1, knot_dev), F32),
        ),
        in_specs=[hbm] * 13,
        out_specs=[vmem] * 8,
        scratch_shapes=[
            pltpu.VMEM(a.shape, a.dtype)
            for a in (
                left_vector,
                source_coeffs,
                knot_coeffs,
                source_index,
                band_start,
                source_vector,
                knot_vector,
            )
        ]
        + [
            pltpu.SMEM((buckets,), jnp.int32),
            pltpu.SMEM((3,), F32),
            pltpu.VMEM((n_src, 8, 128), F32),
            pltpu.VMEM((n_tm, 2, cap), F32),
            pltpu.VMEM((n_tm, 2, cap), F32),
            pltpu.VMEM((n_tm, 1, cap), F32),
            pltpu.VMEM((n_tm, 1, cap), F32),
            pltpu.VMEM((n_src, 8, 128), F32),
            pltpu.VMEM((n_src, 8, 128), F32),
            pltpu.VMEM((17 - 2 * FAR, N_X, 8, 128), F32),
            pltpu.VMEM((2, N_X, 8, 128), F32),
            pltpu.VMEM((n_src, 1, 128), F32),
            pltpu.VMEM((n_tm, 1, 128), F32),
            pltpu.VMEM((N_X * n_tm, 1, 128), F32),
            pltpu.VMEM((n_src // N_X, 1, 128), F32),
            pltpu.VMEM((n_tm, 128, cap), BF16),
            pltpu.VMEM((n_tm, 256, cap), BF16),
            pltpu.VMEM((n_tm, 9, 16, cap), BF16),
            pltpu.SemaphoreType.DMA((13,)),
        ]
        + [pltpu.SemaphoreType.DMA((5,))]
        + [pltpu.SemaphoreType.DMA((3,))] * 7,
        compiler_params=pltpu.CompilerParams(collective_id=0, has_side_effects=True),
    )(
        left_vector,
        source_coeffs,
        knot_coeffs,
        source_index,
        band_start,
        source_vector,
        knot_vector,
        bucket_fill.reshape(buckets),
        recurrence,
        source_search,
        knot_search,
        source_solution,
        knot_solution,
    )
    held = [pltpu.with_memory_space_constraint(v, pltpu.VMEM) for v in held]
    outs = pl.pallas_call(
        finish,
        out_shape=(
            jax.ShapeDtypeStruct((buckets, cap), F32),
            jax.ShapeDtypeStruct((5, source_dev), F32),
            jax.ShapeDtypeStruct((3, 1, knot_dev), F32),
            jax.ShapeDtypeStruct((5, source_dev), F32),
            jax.ShapeDtypeStruct((3, 1, knot_dev), F32),
            jax.ShapeDtypeStruct((5, source_dev), F32),
            jax.ShapeDtypeStruct((3, 1, knot_dev), F32),
            jax.ShapeDtypeStruct((1, 4), F32),
        ),
        in_specs=[vmem] * 8,
        out_specs=[vmem] * 8,
    )(*held)
    return (*outs[:7], outs[7].reshape(4))


def solution(mesh):
    in_specs = (
        P(None, ("src", "tm")),
        P(None, None, ("src", "tm")),
        P(None, None, ("src", "tm")),
        P(None, ("src", "tm")),
        P(None, ("src", "tm")),
        P(None, ("src", "tm")),
        P(None, ("src", "tm")),
        P(None, "tm", "src"),
        P(None, ("src", "tm")),
        P(None, "tm", "src"),
        P(None, ("src", "tm")),
        P(None, "tm", "src"),
        P(),
    )
    out_specs = (
        P(None, ("src", "tm")),
        P(None, ("src", "tm")),
        P(None, "tm", "src"),
        P(None, ("src", "tm")),
        P(None, "tm", "src"),
        P(None, ("src", "tm")),
        P(None, "tm", "src"),
        P(),
    )
    return jax.shard_map(shards, mesh=mesh, in_specs=in_specs, out_specs=out_specs, check_vma=False)
```
